256 devices in a mesh: gene: 4 (over z_hi, core), peak: 64 (over x, z_lo, y).
Axes of the slice: x: 4, y: 4, z: 8 (z_hi: 2, z_lo: 4; z = z_hi * 4 + z_lo), core: 2. Of those that a mesh axis runs over, the one named last changes fastest.
Arguments:
- gene_act: bfloat16 [32768, 1024], P('peak'), may hold values from -6 to 6
- peak_act: bfloat16 [131072, 1024], P('peak'), may hold values from -6 to 6
- w_query: bfloat16 [1024, 1024], P(None, 'gene'), may hold values from -0.1875 to 0.1875
- w_key: bfloat16 [1024, 1024], P(None, 'gene'), may hold values from -0.1875 to 0.1875
- w_value: bfloat16 [1024, 1024], P(None, 'gene'), may hold values from -0.1875 to 0.1875
- w_out: bfloat16 [1024, 1024], P('gene'), may hold values from -0.1875 to 0.1875
- head_bias: float32 [8], P('gene'), may hold values from -6 to -3
- block_mask: int32 [256, 1024], replicated, may hold values from 0 to 1, as said below
- gene_chrom: int32 [32768], replicated, may hold values from 0 to 22, as said below
- peak_chrom: int32 [131072], replicated, may hold values from 0 to 22, as said below
Outputs:
- mixed: bfloat16 [32768, 1024], P('peak', 'gene')
The draws below stay inside these ranges and needn't reach their ends.
Inputs may be any that keep to these rules, and one draw needn't show every extreme that they name: For each gene tile i, the 1s of block_mask[i] form one run of consecutive peak tiles that contains tile 4i and lies within the peak tiles of the shards o - 2 to o + 2, where o = i // 4 is the shard of peak that holds gene tile i; runs of different lengths reach that limit on either side in every draw. `peak_chrom`: never falls along the peaks; each chromosome is one run of consecutive peaks. `gene_chrom`: gene query g lies at peak position 4g and carries that peak's chromosome.
All inputs are finite; a program needn't handle non-finite values.
Results may differ from the reference program's by a relative error of at most 0.0064.
Values may be sent and summed in bfloat16 or wider, within the bound.
No kernel may reach another device: no remote copies, remote signals or barrier semaphores. Data moves between devices by JAX's collectives and lax.ppermute only.
A program may use at most 128 MiB of HBM per device.

```python
import math
import jax
import jax.numpy as jnp
from jax import lax

D = 1024
HEADS = 8
GENE_DEV = 512
PEAK_DEV = 2048
TILE = 128
REACH = 2
CHROMS = 23
GENES = 32768
PEAKS = 131072
GENE_TILES = 256
PEAK_TILES = 1024
N_PEAK = 64


def chromosome_cuts(key):
    spacing = PEAKS // GENES
    return jax.random.randint(jax.random.fold_in(key, 7), (CHROMS - 1,), 1, PEAKS - spacing)


def draw_peak_chrom(key, part):
    cuts = chromosome_cuts(key)
    position = jnp.arange(PEAKS, dtype=jnp.int32)
    return jnp.sum((cuts[None, :] <= position[:, None]).astype(jnp.int32), axis=1)


def draw_gene_chrom(key, part):
    cuts = chromosome_cuts(key)
    position = jnp.arange(GENES, dtype=jnp.int32) * (PEAKS // GENES)
    return jnp.sum((cuts[None, :] <= position[:, None]).astype(jnp.int32), axis=1)


def draw_block_mask(key, part):
    per_dev = PEAK_DEV // TILE
    ratio = PEAK_TILES // GENE_TILES
    row = jnp.arange(GENE_TILES, dtype=jnp.int32)
    owner = row // (GENE_DEV // TILE)
    centre = row * ratio
    reach_low = jax.random.randint(jax.random.fold_in(key, 11), (GENE_TILES,), 0, (REACH + 1) * per_dev + 1)
    reach_high = jax.random.randint(jax.random.fold_in(key, 13), (GENE_TILES,), 0, (REACH + 1) * per_dev + 1)
    lowest = jnp.maximum(centre - reach_low, (owner - REACH) * per_dev)
    highest = jnp.minimum(centre + reach_high, (owner + REACH + 1) * per_dev - 1)
    column = jnp.arange(PEAK_TILES, dtype=jnp.int32)
    inside = (column[None, :] >= lowest[:, None]) & (column[None, :] <= highest[:, None])
    return inside.astype(jnp.int32)


def block_scale(rng, shape, split, smallest, high):
    def one(dim, shards_of):
        draws = jax.random.uniform(jax.random.fold_in(jax.random.fold_in(rng, 6), dim), (shards_of,), jnp.float32, smallest / len(split), high / len(split))
        return jnp.repeat(jnp.exp(draws), shape[dim] // shards_of).reshape((-1,) + (1,) * (len(shape) - dim - 1))

    gain = one(*split[0])
    for cut in split[1:]:
        gain = gain * one(*cut)
    return gain


def centred(stream_key, shape, width, bound, pieces=(), kind=jnp.bfloat16):
    array = jax.random.normal(stream_key, shape, jnp.float32) * width
    if len(pieces) > 0:
        array = block_scale(stream_key, shape, pieces, -0.22, 0.18) * array
    return jnp.clip(array, min=-bound, max=bound).astype(kind)


def setup_inputs(seed: int = 0) -> dict:
    arg_keys = jax.random.split(jax.random.key(seed), 11)
    gene_act = centred(arg_keys[0], (GENES, D), 1.0, 6.0, ((0, 64),))
    peak_act = centred(arg_keys[1], (PEAKS, D), 1.0, 6.0, ((0, 64),))
    w_query = centred(arg_keys[2], (D, D), D ** -0.5, 0.1875, ((1, 4),))
    w_key = centred(arg_keys[3], (D, D), D ** -0.5, 0.1875, ((1, 4),))
    w_value = centred(arg_keys[4], (D, D), D ** -0.5, 0.1875, ((1, 4),))
    w_out = centred(arg_keys[5], (D, D), D ** -0.5, 0.1875, ((0, 4),))
    head_bias = jnp.clip(-6.0 + 3.0 * jax.random.uniform(arg_keys[6], (HEADS,), jnp.float32) ** block_scale(arg_keys[6], (HEADS,), ((0, 4),), -0.2, 0.2), -6.0, -3.0)
    block_mask = draw_block_mask(jax.random.fold_in(arg_keys[10], 71), 0)
    gene_chrom = draw_gene_chrom(jax.random.fold_in(arg_keys[10], 71), 0)
    peak_chrom = draw_peak_chrom(jax.random.fold_in(arg_keys[10], 71), 0)
    return dict(gene_act=gene_act, peak_act=peak_act, w_query=w_query, w_key=w_key, w_value=w_value, w_out=w_out, head_bias=head_bias, block_mask=block_mask, gene_chrom=gene_chrom, peak_chrom=peak_chrom)


def expand_tiles(tiles, tile_rows):
    rows, cols = tiles.shape
    spread = jnp.broadcast_to(tiles.astype(jnp.float32)[:, None, :, None], (rows, tile_rows, cols, tile_rows))
    return spread.reshape(rows * tile_rows, cols * tile_rows)

def reference(gene_act, peak_act, w_query, w_key, w_value, w_out, head_bias, block_mask, gene_chrom, peak_chrom):
    head_dim = D // HEADS
    queries = jnp.dot(gene_act, w_query, preferred_element_type=jnp.float32).astype(jnp.bfloat16).reshape(GENES, HEADS, head_dim)
    keys_all = jnp.dot(peak_act, w_key, preferred_element_type=jnp.float32).astype(jnp.bfloat16).reshape(PEAKS, HEADS, head_dim)
    values_all = jnp.dot(peak_act, w_value, preferred_element_type=jnp.float32).astype(jnp.bfloat16).reshape(PEAKS, HEADS, head_dim)
    margin = REACH * PEAK_DEV
    keys_pad = jnp.pad(keys_all, ((margin, margin), (0, 0), (0, 0)))
    values_pad = jnp.pad(values_all, ((margin, margin), (0, 0), (0, 0)))
    tile_margin = REACH * (PEAK_DEV // TILE)
    mask_pad = jnp.pad(block_mask, ((0, 0), (tile_margin, tile_margin)))
    tag_pad = jnp.pad(peak_chrom, (margin, margin), constant_values=-1)
    window = (2 * REACH + 1) * PEAK_DEV
    gene_tiles = GENE_DEV // TILE
    window_tiles = window // TILE
    peak_tiles = PEAK_DEV // TILE
    scale = 1.0 / math.sqrt(head_dim)

    def one_block(block):
        start = (block * PEAK_DEV).astype(jnp.int32)
        gene_start = (block * GENE_DEV).astype(jnp.int32)
        query_rows = lax.dynamic_slice_in_dim(queries, gene_start, GENE_DEV, 0)
        key_rows = lax.dynamic_slice_in_dim(keys_pad, start, window, 0)
        value_rows = lax.dynamic_slice_in_dim(values_pad, start, window, 0)
        tiles = lax.dynamic_slice(mask_pad, ((block * gene_tiles).astype(jnp.int32), (block * peak_tiles).astype(jnp.int32)), (gene_tiles, window_tiles))
        gene_tag = lax.dynamic_slice_in_dim(gene_chrom, gene_start, GENE_DEV)
        peak_tag = lax.dynamic_slice_in_dim(tag_pad, start, window)
        allowed = expand_tiles(tiles, TILE) * (gene_tag[:, None] == peak_tag[None, :]).astype(jnp.float32)
        scores = jnp.einsum('ghd,phd->hgp', query_rows.astype(jnp.float32), key_rows.astype(jnp.float32))
        scores = scores * scale + head_bias[:, None, None]
        weights = (jax.nn.sigmoid(scores) * allowed[None]).astype(jnp.bfloat16)
        summed = jnp.einsum('hgp,phd->ghd', weights.astype(jnp.float32), value_rows.astype(jnp.float32))
        return summed.astype(jnp.bfloat16)
    attended = lax.map(one_block, jnp.arange(N_PEAK, dtype=jnp.int32))
    attended = attended.reshape(GENES, D)
    return jnp.dot(attended, w_out, preferred_element_type=jnp.float32).astype(jnp.bfloat16)
```

```python
import functools
import math

import jax
import jax.numpy as jnp
from jax import lax
from jax.experimental import pallas as pl
from jax.experimental.pallas import tpu as pltpu
from jax.sharding import PartitionSpec as P

TILE = 128
REACH = 2
CHUNK = 512
HEAD = 8
F32 = jnp.float32
BF16 = jnp.bfloat16
PARAMS = pltpu.CompilerParams(vmem_limit_bytes=16 << 20)
VMEM = pl.BlockSpec(memory_space=pltpu.VMEM)
SMEM = pl.BlockSpec(memory_space=pltpu.SMEM)


def swap_pairs(count, by, kind):
    pairs = []
    for i in range(count - by):
        if (i // by) % 2 == kind:
            pairs += [(i, i + by), (i + by, i)]
    return pairs


def cost(flops, arrays):
    return pl.CostEstimate(
        flops=flops, bytes_accessed=sum(a.size * a.dtype.itemsize for a in arrays), transcendentals=0
    )


def kv_kernel(act_ref, wk_ref, wv_ref, k_ref, v_ref):
    act = act_ref[...]
    k_ref[...] = jnp.dot(act, wk_ref[...], preferred_element_type=F32).astype(BF16)
    v_ref[...] = jnp.dot(act, wv_ref[...], preferred_element_type=F32).astype(BF16)


def project_kv(act, wk, wv, rows):
    total, depth = act.shape
    width = wk.shape[1]
    whole = pl.BlockSpec((depth, width), lambda i: (0, 0))
    return pl.pallas_call(
        kv_kernel,
        grid=(total // rows,),
        in_specs=[pl.BlockSpec((rows, depth), lambda i: (i, 0)), whole, whole],
        out_specs=[pl.BlockSpec((rows, width), lambda i: (i, 0))] * 2,
        out_shape=[jax.ShapeDtypeStruct((total, width), BF16)] * 2,
        cost_estimate=cost(4 * total * depth * width, [act, wk, wv, act]),
        compiler_params=PARAMS,
        name="project_kv",
    )(act, wk, wv)


def attend_kernel(slot, heads, meta_ref, bias_ref, gene_ref, peak_ref, q_ref, k_ref, v_ref, o_ref, acc):
    tiles = q_ref.shape[0] // TILE
    per_chunk = CHUNK // TILE
    dim = q_ref.shape[1] // heads
    scale = 0.5 / math.sqrt(dim)
    start = meta_ref[slot]
    base = jnp.maximum(start, 0)
    lows = [meta_ref[HEAD + 2 * (base + i)] for i in range(tiles)]
    highs = [meta_ref[HEAD + 2 * (base + i) + 1] for i in range(tiles)]
    low = functools.reduce(jnp.minimum, lows)
    high = functools.reduce(jnp.maximum, highs)
    first = low // per_chunk
    last = jnp.where(start < 0, first, (high + per_chunk - 1) // per_chunk)
    acc[...] = jnp.zeros_like(acc)
    tags = [
        jnp.broadcast_to(gene_ref[pl.ds(base + i, 1), :], (TILE, TILE)).T for i in range(tiles)
    ]

    def chunk(c, carry):
        rows = pl.ds(pl.multiple_of(c * CHUNK, CHUNK), CHUNK)
        peaks = [peak_ref[pl.ds(c * per_chunk + j, 1), :] for j in range(per_chunk)]
        for h in range(heads):
            cols = slice(h * dim, (h + 1) * dim)
            scores = lax.dot_general(
                q_ref[:, cols], k_ref[rows, cols], (((1,), (1,)), ((), ())), preferred_element_type=F32
            )
            twice = jnp.tanh(scores * scale + 0.5 * bias_ref[h]) + 1.0
            bands = []
            for i in range(tiles):
                band = []
                for j in range(per_chunk):
                    t = c * per_chunk + j
                    inside = (t >= lows[i]) & (t < highs[i])
                    allowed = tags[i] == jnp.where(inside, peaks[j], -1)
                    part = twice[i * TILE : (i + 1) * TILE, j * TILE : (j + 1) * TILE]
                    band.append(jnp.where(allowed, part, 0.0))
                bands.append(jnp.concatenate(band, 1))
            weights = jnp.concatenate(bands, 0).astype(BF16)
            acc[:, cols] += jnp.dot(weights, v_ref[rows, cols], preferred_element_type=F32)
        return carry

    lax.fori_loop(first, last, chunk, 0)
    o_ref[...] = (acc[...] * 0.5).astype(o_ref.dtype)


def attend(slot, heads, meta, bias, gene, peak, q, k, v, dtype):
    return pl.pallas_call(
        functools.partial(attend_kernel, slot, heads),
        in_specs=[SMEM, SMEM] + [VMEM] * 5,
        out_specs=VMEM,
        out_shape=jax.ShapeDtypeStruct(q.shape, dtype),
        scratch_shapes=[pltpu.VMEM(q.shape, F32)],
        cost_estimate=cost(4 * q.shape[0] * k.shape[0] * k.shape[1], [q, k, v, q]),
        compiler_params=PARAMS,
        name="attend_%d" % slot,
    )(meta, bias, gene, peak, q, k, v)


def mix_kernel(slot, meta_ref, own_ref, r1, r2, r3, r4, w_ref, send_ref, keep_ref):
    width = w_ref.shape[1] // 4
    me = meta_ref[slot]
    total = own_ref[...]
    for r in (r1, r2, r3, r4):
        total = total + r[...].astype(F32)
    attended = total.astype(BF16)

    def share(block):
        cols = pl.ds(pl.multiple_of(block * width, width), width)
        return jnp.dot(attended, w_ref[:, cols], preferred_element_type=F32)

    send_ref[:, :width] = share(me ^ 3).astype(BF16)
    send_ref[:, width:] = share(me ^ 1).astype(BF16)
    keep_ref[:, :width] = share(me ^ 2)
    keep_ref[:, width:] = share(me)


def mix(slot, meta, own, parts, w):
    shape = (own.shape[0], w.shape[1] // 2)
    return pl.pallas_call(
        functools.partial(mix_kernel, slot),
        in_specs=[SMEM] + [VMEM] * 6,
        out_specs=[VMEM, VMEM],
        out_shape=[jax.ShapeDtypeStruct(shape, BF16), jax.ShapeDtypeStruct(shape, F32)],
        cost_estimate=cost(2 * own.shape[0] * w.size, [own, w, own, own]),
        compiler_params=PARAMS,
        name="mix",
    )(meta, own, *parts, w)


def on_device(
    gene_act,
    peak_act,
    w_query,
    w_key,
    w_value,
    w_out,
    head_bias,
    block_mask,
    gene_chrom,
    peak_chrom,
):
    gene_rows = gene_act.shape[0]
    peak_rows = peak_act.shape[0]
    heads = head_bias.shape[0]
    gene_tiles = gene_rows // TILE
    peak_tiles = peak_rows // TILE
    window = (2 * REACH + 1) * gene_tiles
    me = lax.axis_index("peak")
    count = lax.axis_size("peak")
    gene_me = lax.axis_index("gene")

    queries = jnp.dot(gene_act, w_query, preferred_element_type=F32).astype(BF16)
    steps = [(1, 1), (2, 1), (1, 0), (2, 0)]
    far = [lax.ppermute(queries, "peak", swap_pairs(count, by, kind)) for by, kind in steps]

    origin = jnp.clip((me - REACH) * gene_tiles, 0, count * gene_tiles - window)
    tiles = lax.dynamic_slice(block_mask, (origin, me * peak_tiles), (window, peak_tiles))
    gene = lax.dynamic_slice_in_dim(gene_chrom, origin * TILE, window * TILE).reshape(window, TILE)
    peak = lax.dynamic_slice_in_dim(peak_chrom, me * peak_rows, peak_rows).reshape(peak_tiles, TILE)
    meet = (gene[:, :1] <= peak[None, :, -1]) & (peak[None, :, 0] <= gene[:, -1:])
    live = (tiles > 0) & meet
    place = lax.broadcasted_iota(jnp.int32, live.shape, 1)
    low = jnp.min(jnp.where(live, place, peak_tiles), axis=1)
    high = jnp.max(jnp.where(live, place + 1, 0), axis=1)
    words = []
    for by, kind in [(0, 0)] + steps:
        if by:
            by = jnp.where((me // by) % 2 == kind, by, -by)
        source = me + by
        inside = (source >= 0) & (source < count)
        words.append(jnp.where(inside, source * gene_tiles - origin, -1))
    words.append(gene_me)
    words += [jnp.zeros_like(gene_me)] * (HEAD - len(words))
    meta = jnp.concatenate([jnp.stack(words), jnp.stack([low, high], 1).reshape(-1)]).astype(jnp.int32)

    keys, values = project_kv(peak_act, w_key, w_value, 512)
    own = attend(0, heads, meta, head_bias, gene, peak, queries, keys, values, F32)
    parts = []
    for slot, (by, kind) in enumerate(steps):
        part = attend(slot + 1, heads, meta, head_bias, gene, peak, far[slot], keys, values, BF16)
        parts.append(lax.ppermute(part, "peak", swap_pairs(count, by, kind)))
    send, keep = mix(len(steps) + 1, meta, own, parts, w_out)
    width = send.shape[1] // 2
    heard = lax.ppermute(send, "gene", [(0, 1), (1, 0), (2, 3), (3, 2)])
    half = keep + heard.astype(F32)
    other = lax.ppermute(half[:, :width].astype(BF16), "gene", [(0, 2), (2, 0), (1, 3), (3, 1)])
    return (half[:, width:] + other.astype(F32)).astype(BF16)


def solution(mesh):
    placed = (
        P("peak", None),
        P("peak", None),
        P(None, "gene"),
        P(None, "gene"),
        P(None, "gene"),
        P("gene", None),
        P("gene"),
        P(),
        P(),
        P(),
    )
    return jax.shard_map(
        on_device, mesh=mesh, in_specs=placed, out_specs=P("peak", "gene"), check_vma=False
    )
```

```python
import functools
import math

import jax
import jax.numpy as jnp
from jax import lax
from jax.experimental import pallas as pl
from jax.experimental.pallas import tpu as pltpu
from jax.sharding import PartitionSpec as P


TILE = 128
REACH = 2
CHUNK = 512
SPAN = 32
F32 = jnp.float32
BF16 = jnp.bfloat16
I32 = jnp.int32
VMEM = pl.BlockSpec(memory_space=pltpu.VMEM)
SMEM = pl.BlockSpec(memory_space=pltpu.SMEM)
ANY = pl.BlockSpec(memory_space=pl.ANY)
PARAMS = pltpu.CompilerParams(vmem_limit_bytes=20 << 20)


def swap_pairs(genes, count, by):
    pairs = []
    for g in range(genes):
        for i in range(count - by):
            if (i // by) % 2 == g % 2:
                a, b = g * count + i, g * count + i + by
                pairs += [(a, b), (b, a)]
    return pairs


def core_swap(x):
    return lax.ppermute(x, "gene", [(0, 1), (1, 0), (2, 3), (3, 2)])


def cost(flops, arrays):
    return pl.CostEstimate(
        flops=flops, bytes_accessed=sum(a.size * a.dtype.itemsize for a in arrays), transcendentals=0
    )


def window_origin(gene_tiles):
    me, count = lax.axis_index("peak"), lax.axis_size("peak")
    first = jnp.maximum((me - REACH) * gene_tiles, 0)
    return jnp.minimum((first // 8) * 8, count * gene_tiles - SPAN)


def query_kernel(act_ref, w_ref, q_ref):
    q_ref[...] = jnp.dot(act_ref[...], w_ref[...], preferred_element_type=F32).astype(BF16)


def query_join_kernel(act_ref, w_ref, own_ref, q_ref):
    width = w_ref.shape[1]
    q_ref[:, :width] = own_ref[...]
    q_ref[:, width:] = jnp.dot(act_ref[...], w_ref[...], preferred_element_type=F32).astype(BF16)


def project_queries(act, own, other):
    rows, width = act.shape[0], own.shape[1]
    half = pl.pallas_call(
        query_kernel,
        in_specs=[VMEM] * 2,
        out_specs=VMEM,
        out_shape=jax.ShapeDtypeStruct((rows, width), BF16),
        cost_estimate=cost(2 * act.size * width, [act, own]),
        name="project_queries",
    )(act, own)
    return pl.pallas_call(
        query_join_kernel,
        in_specs=[VMEM] * 3,
        out_specs=VMEM,
        out_shape=jax.ShapeDtypeStruct((rows, 2 * width), BF16),
        cost_estimate=cost(8_000_000_000, [act, own]),
        compiler_params=PARAMS,
        name="join_queries",
    )(act, other, half)


def kv_kernel(
    gene_tiles, act_ref, wk1, wk2, wv1, wv2, mask_hbm, gene_hbm, peak_hbm,
    k_ref, v_ref, runs_ref, gene_ref, peak_ref, mask_ref, turned_ref, sems,
):
    me = lax.axis_index("peak")
    tiles = peak_ref.shape[0]
    origin = pl.multiple_of(window_origin(gene_tiles), 8)
    per_block = TILE // tiles
    columns = pl.multiple_of((me // per_block) * TILE, TILE)
    copies = [
        pltpu.make_async_copy(
            mask_hbm.at[pl.ds(origin, SPAN), pl.ds(columns, TILE)], mask_ref, sems.at[0]
        ),
        pltpu.make_async_copy(gene_hbm.at[pl.ds(origin, SPAN), :], gene_ref, sems.at[1]),
        pltpu.make_async_copy(
            peak_hbm.at[pl.ds(pl.multiple_of(me * tiles, 8), tiles), :], peak_ref, sems.at[2]
        ),
    ]
    for copy in copies:
        copy.start()
    width = wk1.shape[1]

    def block(i, carry):
        rows = pl.ds(pl.multiple_of(i * CHUNK, CHUNK), CHUNK)
        act = act_ref[rows, :]
        k_ref[rows, :width] = jnp.dot(act, wk1[...], preferred_element_type=F32).astype(BF16)
        v_ref[rows, :width] = jnp.dot(act, wv1[...], preferred_element_type=F32).astype(BF16)
        k_ref[rows, width:] = jnp.dot(act, wk2[...], preferred_element_type=F32).astype(BF16)
        v_ref[rows, width:] = jnp.dot(act, wv2[...], preferred_element_type=F32).astype(BF16)
        return carry

    lax.fori_loop(0, act_ref.shape[0] // CHUNK, block, 0)
    for copy in copies:
        copy.wait()
    blank = jnp.zeros((TILE - SPAN, TILE), I32)
    turned_ref[...] = jnp.concatenate([mask_ref[...], blank], 0).T
    allowed = turned_ref[pl.ds(pl.multiple_of((me % per_block) * tiles, 8), tiles), :]
    tags = jnp.concatenate([gene_ref[...], blank], 0).T
    peak = peak_ref[...]
    live = (
        (allowed > 0) & (tags[:1, :] <= peak[:, TILE - 1 :]) & (peak[:, :1] <= tags[TILE - 1 :, :])
    )
    place = lax.broadcasted_iota(I32, live.shape, 0)
    runs_ref[...] = jnp.zeros_like(runs_ref)
    runs_ref[0:1, :] = jnp.min(jnp.where(live, place, tiles), axis=0, keepdims=True)
    runs_ref[1:2, :] = jnp.max(jnp.where(live, place + 1, 0), axis=0, keepdims=True)


def project_kv(gene_tiles, act, wk, wv, mask, gene, peak):
    total, depth = act.shape
    width = 2 * wk[0].shape[1]
    tiles = total // TILE
    return pl.pallas_call(
        functools.partial(kv_kernel, gene_tiles),
        in_specs=[VMEM] * 5 + [ANY] * 3,
        out_specs=[VMEM] * 5,
        out_shape=[
            jax.ShapeDtypeStruct((total, width), BF16),
            jax.ShapeDtypeStruct((total, width), BF16),
            jax.ShapeDtypeStruct((8, TILE), I32),
            jax.ShapeDtypeStruct((SPAN, TILE), I32),
            jax.ShapeDtypeStruct((tiles, TILE), I32),
        ],
        scratch_shapes=[
            pltpu.VMEM((SPAN, TILE), I32),
            pltpu.VMEM((TILE, TILE), I32),
            pltpu.SemaphoreType.DMA((3,)),
        ],
        cost_estimate=cost(4 * total * depth * width, [act, act]),
        compiler_params=PARAMS,
        name="project_kv",
    )(act, *wk, *wv, mask, gene, peak)


def attend_kernel(
    by, heads, runs_ref, own_bias, other_bias, gene_ref, peak_ref, q_ref, k_ref, v_ref, o_ref, acc
):
    tiles = q_ref.shape[0] // TILE
    per_chunk = CHUNK // TILE
    dim = TILE
    scale = 0.5 / math.sqrt(dim)
    me, count = lax.axis_index("peak"), lax.axis_size("peak")
    source = me
    if by:
        kind = lax.axis_index("gene") % 2
        source = jnp.where((me // by) % 2 == kind, me + by, me - by)
    valid = (source >= 0) & (source < count)
    base = jnp.where(valid, source * tiles - window_origin(tiles), 0)
    lows = [runs_ref[0, base + i] for i in range(tiles)]
    highs = [runs_ref[1, base + i] for i in range(tiles)]
    low = functools.reduce(jnp.minimum, lows)
    high = functools.reduce(jnp.maximum, highs)
    first = low // per_chunk
    last = jnp.where(valid, (high + per_chunk - 1) // per_chunk, first)
    acc[...] = jnp.zeros_like(acc)
    tags = [
        jnp.broadcast_to(gene_ref[pl.ds(base + i, 1), :], (TILE, TILE)).T for i in range(tiles)
    ]
    local = own_bias.shape[0]

    def chunk(c, carry):
        rows = pl.ds(pl.multiple_of(c * CHUNK, CHUNK), CHUNK)
        peaks = [peak_ref[pl.ds(c * per_chunk + j, 1), :] for j in range(per_chunk)]
        inside = [
            [
                jnp.where((c * per_chunk + j >= lows[i]) & (c * per_chunk + j < highs[i]), peaks[j], -1)
                for j in range(per_chunk)
            ]
            for i in range(tiles)
        ]
        for h in range(heads):
            cols = slice(h * dim, (h + 1) * dim)
            bias = own_bias[h] if h < local else other_bias[h - local]
            scores = lax.dot_general(
                q_ref[:, cols], k_ref[rows, cols], (((1,), (1,)), ((), ())), preferred_element_type=F32
            )
            twice = jnp.tanh(scores * scale + 0.5 * bias) + 1.0
            bands = []
            for i in range(tiles):
                band = []
                for j in range(per_chunk):
                    part = twice[i * TILE : (i + 1) * TILE, j * TILE : (j + 1) * TILE]
                    band.append(jnp.where(tags[i] == inside[i][j], part, 0.0))
                bands.append(jnp.concatenate(band, 1))
            weights = jnp.concatenate(bands, 0).astype(BF16)
            acc[:, cols] += jnp.dot(weights, v_ref[rows, cols], preferred_element_type=F32)
        return carry

    lax.fori_loop(first, last, chunk, 0)
    o_ref[...] = (acc[...] * 0.5).astype(o_ref.dtype)


def attend(by, heads, tables, q, k, v, dtype):
    runs, own_bias, other_bias, gene, peak = tables
    shape = (q.shape[0], heads * TILE)
    return pl.pallas_call(
        functools.partial(attend_kernel, by, heads),
        in_specs=[SMEM] * 3 + [VMEM] * 5,
        out_specs=VMEM,
        out_shape=jax.ShapeDtypeStruct(shape, dtype),
        scratch_shapes=[pltpu.VMEM(shape, F32)],
        cost_estimate=cost(4 * q.shape[0] * k.shape[0] * heads * TILE, [q, k, v, q]),
        compiler_params=PARAMS,
    )(runs, own_bias, other_bias, gene, peak, q, k, v)


def mix_kernel(own_ref, near_ref, far_ref, w1, w2, send_ref, keep_ref):
    width = w1.shape[1] // 4
    depth = w1.shape[0]
    me = lax.axis_index("gene")
    mine = own_ref[...] + near_ref[:, :depth].astype(F32) + far_ref[:, :depth].astype(F32)
    theirs = near_ref[:, depth:].astype(F32) + far_ref[:, depth:].astype(F32)
    mine, theirs = mine.astype(BF16), theirs.astype(BF16)

    def share(block):
        cols = pl.ds(pl.multiple_of(block * width, width), width)
        return jnp.dot(mine, w1[:, cols], preferred_element_type=F32) + jnp.dot(
            theirs, w2[:, cols], preferred_element_type=F32
        )

    send_ref[:, :width] = share(me ^ 3).astype(BF16)
    send_ref[:, width:] = share(me ^ 1).astype(BF16)
    keep_ref[:, :width] = share(me ^ 2)
    keep_ref[:, width:] = share(me)


def mix(own, near, far, w1, w2):
    shape = (own.shape[0], w1.shape[1] // 2)
    return pl.pallas_call(
        mix_kernel,
        in_specs=[VMEM] * 5,
        out_specs=[VMEM, VMEM],
        out_shape=[jax.ShapeDtypeStruct(shape, BF16), jax.ShapeDtypeStruct(shape, F32)],
        cost_estimate=cost(4 * own.shape[0] * w1.size, [own, w1, w2, own, own]),
        compiler_params=PARAMS,
        name="mix",
    )(own, near, far, w1, w2)


def on_device(
    gene_act,
    peak_act,
    w_query,
    w_key,
    w_value,
    w_out,
    head_bias,
    block_mask,
    gene_chrom,
    peak_chrom,
):
    gene_tiles = gene_act.shape[0] // TILE
    local = head_bias.shape[0]
    count, genes = lax.axis_size("peak"), lax.axis_size("gene")

    def travel(x, by):
        return lax.ppermute(x, ("gene", "peak"), swap_pairs(genes, count, by))

    queries = project_queries(gene_act, w_query, core_swap(w_query))
    near, far = travel(queries, 1), travel(queries, 2)
    keys, values, runs, gene, peak = project_kv(
        gene_tiles,
        peak_act,
        (w_key, core_swap(w_key)),
        (w_value, core_swap(w_value)),
        block_mask,
        gene_chrom.reshape(-1, TILE),
        peak_chrom.reshape(-1, TILE),
    )
    tables = (runs, head_bias, core_swap(head_bias), gene, peak)
    near = travel(attend(1, 2 * local, tables, near, keys, values, BF16), 1)
    far = travel(attend(2, 2 * local, tables, far, keys, values, BF16), 2)
    own = attend(0, local, tables, queries, keys, values, F32)
    send, keep = mix(own, near, far, w_out, core_swap(w_out))
    width = send.shape[1] // 2
    half = keep + core_swap(send).astype(F32)
    other = lax.ppermute(half[:, :width].astype(BF16), "gene", [(0, 2), (2, 0), (1, 3), (3, 1)])
    return (half[:, width:] + other.astype(F32)).astype(BF16)


def solution(mesh):
    placed = (
        P("peak", None),
        P("peak", None),
        P(None, "gene"),
        P(None, "gene"),
        P(None, "gene"),
        P("gene", None),
        P("gene"),
        P(),
        P(),
        P(),
    )
    return jax.shard_map(
        on_device, mesh=mesh, in_specs=placed, out_specs=P("peak", "gene"), check_vma=False
    )
```

```python
import functools
import math

import jax
import jax.numpy as jnp
from jax import lax
from jax.experimental import pallas as pl
from jax.experimental.pallas import tpu as pltpu
from jax.sharding import PartitionSpec as P


TILE = 128
REACH = 2
CHUNK = 512
SPAN = 32
BYS = (2, 1)
CROSSED = True
F32 = jnp.float32
BF16 = jnp.bfloat16
I32 = jnp.int32
VMEM = pl.BlockSpec(memory_space=pltpu.VMEM)
SMEM = pl.BlockSpec(memory_space=pltpu.SMEM)
HBM = pl.BlockSpec(memory_space=pltpu.HBM)
PARAMS = pltpu.CompilerParams(vmem_limit_bytes=20 << 20)


def partner_kind(core, turn):
    by = BYS[turn]
    return by, (core ^ (by - 1)) if CROSSED else core


def swap_pairs(genes, count, turn):
    pairs = []
    for g in range(genes):
        by, kind = partner_kind(g % 2, turn)
        for i in range(count - by):
            if (i // by) % 2 == kind:
                a, b = g * count + i, g * count + i + by
                pairs += [(a, b), (b, a)]
    return pairs


def core_swap(x):
    return lax.ppermute(x, "gene", [(0, 1), (1, 0), (2, 3), (3, 2)])


def cost(flops, arrays):
    return pl.CostEstimate(
        flops=flops, bytes_accessed=sum(a.size * a.dtype.itemsize for a in arrays), transcendentals=0
    )


def window_origin(gene_tiles):
    me, count = lax.axis_index("peak"), lax.axis_size("peak")
    first = jnp.maximum((me - REACH) * gene_tiles, 0)
    return jnp.minimum((first // 8) * 8, count * gene_tiles - SPAN)


def query_kernel(act_ref, w_ref, q_ref):
    q_ref[...] = jnp.dot(act_ref[...], w_ref[...], preferred_element_type=F32).astype(BF16)


def query_join_kernel(act_ref, w_ref, own_ref, q_ref):
    width = w_ref.shape[1]
    q_ref[:, :width] = own_ref[...]
    q_ref[:, width:] = jnp.dot(act_ref[...], w_ref[...], preferred_element_type=F32).astype(BF16)


def project_queries(act, own, other):
    rows, width = act.shape[0], own.shape[1]
    half = pl.pallas_call(
        query_kernel,
        in_specs=[VMEM] * 2,
        out_specs=VMEM,
        out_shape=jax.ShapeDtypeStruct((rows, width), BF16),
        cost_estimate=cost(2 * act.size * width, [act, own]),
        compiler_params=PARAMS,
        name="project_queries",
    )(act, own)
    return pl.pallas_call(
        query_join_kernel,
        in_specs=[VMEM] * 3,
        out_specs=VMEM,
        out_shape=jax.ShapeDtypeStruct((rows, 2 * width), BF16),
        cost_estimate=cost(8_000_000_000, [act, own]),
        compiler_params=PARAMS,
        name="join_queries",
    )(act, other, half)


def kv_kernel(
    gene_tiles, act_ref, wk1, wk2, wv1, wv2, mask_hbm, gene_hbm, peak_hbm,
    k_ref, v_ref, runs_ref, gene_ref, peak_ref, mask_ref, turned_ref, sems,
):
    me = lax.axis_index("peak")
    tiles = peak_ref.shape[0]
    origin = pl.multiple_of(window_origin(gene_tiles), 8)
    per_block = TILE // tiles
    columns = pl.multiple_of((me // per_block) * TILE, TILE)
    copies = [
        pltpu.make_async_copy(
            mask_hbm.at[pl.ds(origin, SPAN), pl.ds(columns, TILE)], mask_ref, sems.at[0]
        ),
        pltpu.make_async_copy(gene_hbm.at[pl.ds(origin, SPAN), :], gene_ref, sems.at[1]),
        pltpu.make_async_copy(
            peak_hbm.at[pl.ds(pl.multiple_of(me * tiles, 8), tiles), :], peak_ref, sems.at[2]
        ),
    ]
    for copy in copies:
        copy.start()
    width = wk1.shape[1]

    def block(i, carry):
        rows = pl.ds(pl.multiple_of(i * CHUNK, CHUNK), CHUNK)
        act = act_ref[rows, :]
        k_ref[rows, :width] = jnp.dot(act, wk1[...], preferred_element_type=F32).astype(BF16)
        v_ref[rows, :width] = jnp.dot(act, wv1[...], preferred_element_type=F32).astype(BF16)
        k_ref[rows, width:] = jnp.dot(act, wk2[...], preferred_element_type=F32).astype(BF16)
        v_ref[rows, width:] = jnp.dot(act, wv2[...], preferred_element_type=F32).astype(BF16)
        return carry

    lax.fori_loop(0, act_ref.shape[0] // CHUNK, block, 0)
    for copy in copies:
        copy.wait()
    blank = jnp.zeros((TILE - SPAN, TILE), I32)
    turned_ref[...] = jnp.concatenate([mask_ref[...], blank], 0).T
    allowed = turned_ref[pl.ds(pl.multiple_of((me % per_block) * tiles, 8), tiles), :]
    tags = jnp.concatenate([gene_ref[...], blank], 0).T
    peak = peak_ref[...]
    live = (
        (allowed > 0) & (tags[:1, :] <= peak[:, TILE - 1 :]) & (peak[:, :1] <= tags[TILE - 1 :, :])
    )
    place = lax.broadcasted_iota(I32, live.shape, 0)
    runs_ref[...] = jnp.zeros_like(runs_ref)
    runs_ref[0:1, :] = jnp.min(jnp.where(live, place, tiles), axis=0, keepdims=True)
    runs_ref[1:2, :] = jnp.max(jnp.where(live, place + 1, 0), axis=0, keepdims=True)


def project_kv(gene_tiles, act, wk, wv, mask, gene, peak):
    total, depth = act.shape
    width = 2 * wk[0].shape[1]
    tiles = total // TILE
    return pl.pallas_call(
        functools.partial(kv_kernel, gene_tiles),
        in_specs=[VMEM] * 5 + [HBM] * 3,
        out_specs=[VMEM] * 5,
        out_shape=[
            jax.ShapeDtypeStruct((total, width), BF16),
            jax.ShapeDtypeStruct((total, width), BF16),
            jax.ShapeDtypeStruct((8, TILE), I32),
            jax.ShapeDtypeStruct((SPAN, TILE), I32),
            jax.ShapeDtypeStruct((tiles, TILE), I32),
        ],
        scratch_shapes=[
            pltpu.VMEM((SPAN, TILE), I32),
            pltpu.VMEM((TILE, TILE), I32),
            pltpu.SemaphoreType.DMA((3,)),
        ],
        cost_estimate=cost(4 * total * depth * width, [act, act]),
        compiler_params=PARAMS,
        name="project_kv",
    )(act, *wk, *wv, mask, gene, peak)


def attend_kernel(
    turn, heads, runs_ref, own_bias, other_bias, gene_ref, peak_ref, q_ref, k_ref, v_ref, o_ref, acc
):
    tiles = q_ref.shape[0] // TILE
    per_chunk = CHUNK // TILE
    dim = TILE
    scale = 0.5 / math.sqrt(dim)
    me, count = lax.axis_index("peak"), lax.axis_size("peak")
    source = me
    if turn is not None:
        by, kind = partner_kind(lax.axis_index("gene") & 1, turn)
        source = jnp.where((me // by) % 2 == kind, me + by, me - by)
    valid = (source >= 0) & (source < count)
    base = jnp.where(valid, source * tiles - window_origin(tiles), 0)
    lows = [runs_ref[0, base + i] for i in range(tiles)]
    highs = [runs_ref[1, base + i] for i in range(tiles)]
    low = functools.reduce(jnp.minimum, lows)
    high = functools.reduce(jnp.maximum, highs)
    first = low // per_chunk
    last = jnp.where(valid, (high + per_chunk - 1) // per_chunk, first)
    acc[...] = jnp.zeros_like(acc)
    tags = [
        jnp.broadcast_to(gene_ref[pl.ds(base + i, 1), :], (TILE, TILE)).T for i in range(tiles)
    ]
    local = own_bias.shape[0]

    def chunk(c, carry):
        rows = pl.ds(pl.multiple_of(c * CHUNK, CHUNK), CHUNK)
        peaks = [peak_ref[pl.ds(c * per_chunk + j, 1), :] for j in range(per_chunk)]
        inside = [
            [
                jnp.where((c * per_chunk + j >= lows[i]) & (c * per_chunk + j < highs[i]), peaks[j], -1)
                for j in range(per_chunk)
            ]
            for i in range(tiles)
        ]
        for h in range(heads):
            cols = slice(h * dim, (h + 1) * dim)
            bias = own_bias[h] if h < local else other_bias[h - local]
            scores = lax.dot_general(
                q_ref[:, cols], k_ref[rows, cols], (((1,), (1,)), ((), ())), preferred_element_type=F32
            )
            twice = jnp.tanh(scores * scale + 0.5 * bias) + 1.0
            bands = []
            for i in range(tiles):
                band = []
                for j in range(per_chunk):
                    part = twice[i * TILE : (i + 1) * TILE, j * TILE : (j + 1) * TILE]
                    band.append(jnp.where(tags[i] == inside[i][j], part, 0.0))
                bands.append(jnp.concatenate(band, 1))
            weights = jnp.concatenate(bands, 0).astype(BF16)
            acc[:, cols] += jnp.dot(weights, v_ref[rows, cols], preferred_element_type=F32)
        return carry

    lax.fori_loop(first, last, chunk, 0)
    o_ref[...] = (acc[...] * 0.5).astype(o_ref.dtype)


def attend(turn, heads, tables, q, k, v, dtype):
    runs, own_bias, other_bias, gene, peak = tables
    shape = (q.shape[0], heads * TILE)
    return pl.pallas_call(
        functools.partial(attend_kernel, turn, heads),
        in_specs=[SMEM] * 3 + [VMEM] * 5,
        out_specs=VMEM,
        out_shape=jax.ShapeDtypeStruct(shape, dtype),
        scratch_shapes=[pltpu.VMEM(shape, F32)],
        cost_estimate=cost(4 * q.shape[0] * k.shape[0] * heads * TILE, [q, k, v, q]),
        compiler_params=PARAMS,
    )(runs, own_bias, other_bias, gene, peak, q, k, v)


def mix_kernel(own_ref, first_ref, second_ref, w1, w2, send_ref, keep_ref):
    width = w1.shape[1] // 4
    depth = w1.shape[0]
    me = lax.axis_index("gene")
    mine = own_ref[...] + first_ref[:, :depth].astype(F32) + second_ref[:, :depth].astype(F32)
    theirs = first_ref[:, depth:].astype(F32) + second_ref[:, depth:].astype(F32)
    mine, theirs = mine.astype(BF16), theirs.astype(BF16)

    def share(block):
        cols = pl.ds(pl.multiple_of(block * width, width), width)
        return jnp.dot(mine, w1[:, cols], preferred_element_type=F32) + jnp.dot(
            theirs, w2[:, cols], preferred_element_type=F32
        )

    send_ref[:, :width] = share(me ^ 3).astype(BF16)
    send_ref[:, width:] = share(me ^ 1).astype(BF16)
    keep_ref[:, :width] = share(me ^ 2)
    keep_ref[:, width:] = share(me)


def mix(own, first, second, w1, w2):
    shape = (own.shape[0], w1.shape[1] // 2)
    return pl.pallas_call(
        mix_kernel,
        in_specs=[VMEM] * 5,
        out_specs=[VMEM, VMEM],
        out_shape=[jax.ShapeDtypeStruct(shape, BF16), jax.ShapeDtypeStruct(shape, F32)],
        cost_estimate=cost(4 * own.shape[0] * w1.size, [own, w1, w2, own, own]),
        compiler_params=PARAMS,
        name="mix",
    )(own, first, second, w1, w2)


def on_device(
    gene_act,
    peak_act,
    w_query,
    w_key,
    w_value,
    w_out,
    head_bias,
    block_mask,
    gene_chrom,
    peak_chrom,
):
    gene_tiles = gene_act.shape[0] // TILE
    local = head_bias.shape[0]
    count, genes = lax.axis_size("peak"), lax.axis_size("gene")

    def travel(x, turn):
        return lax.ppermute(x, ("gene", "peak"), swap_pairs(genes, count, turn))

    queries = project_queries(gene_act, w_query, core_swap(w_query))
    first, second = travel(queries, 0), travel(queries, 1)
    w_key = (w_key, core_swap(w_key))
    w_value = (w_value, core_swap(w_value))
    gene, peak = gene_chrom.reshape(-1, TILE), peak_chrom.reshape(-1, TILE)
    keys, values, runs, gene, peak = project_kv(
        gene_tiles, peak_act, w_key, w_value, block_mask, gene, peak
    )
    tables = (runs, head_bias, core_swap(head_bias), gene, peak)
    first = attend(0, 2 * local, tables, first, keys, values, BF16)
    second = attend(1, 2 * local, tables, second, keys, values, BF16)
    first, second = travel(first, 0), travel(second, 1)
    own = attend(None, local, tables, queries, keys, values, F32)
    send, keep = mix(own, first, second, w_out, core_swap(w_out))
    width = send.shape[1] // 2
    half = keep + core_swap(send).astype(F32)
    other = lax.ppermute(half[:, :width].astype(BF16), "gene", [(0, 2), (2, 0), (1, 3), (3, 1)])
    return (half[:, width:] + other.astype(F32)).astype(BF16)


def solution(mesh):
    placed = (
        P("peak", None),
        P("peak", None),
        P(None, "gene"),
        P(None, "gene"),
        P(None, "gene"),
        P("gene", None),
        P("gene"),
        P(),
        P(),
        P(),
    )
    return jax.shard_map(
        on_device, mesh=mesh, in_specs=placed, out_specs=P("peak", "gene"), check_vma=False
    )
```

```python
import functools
import math

import jax
import jax.numpy as jnp
from jax import lax
from jax.experimental import pallas as pl
from jax.experimental.pallas import tpu as pltpu
from jax.sharding import PartitionSpec as P


TILE = 128
REACH = 2
CHUNK = 512
SPAN = 32
BYS = (2, 1)
CROSSED = True
PARTS = 2
F32 = jnp.float32
BF16 = jnp.bfloat16
I32 = jnp.int32
VMEM = pl.BlockSpec(memory_space=pltpu.VMEM)
SMEM = pl.BlockSpec(memory_space=pltpu.SMEM)
HBM = pl.BlockSpec(memory_space=pltpu.HBM)
PARAMS = pltpu.CompilerParams(vmem_limit_bytes=20 << 20)


def partner_kind(core, turn):
    by = BYS[turn]
    return by, (core ^ (by - 1)) if CROSSED else core


def swap_pairs(genes, count, turn):
    pairs = []
    for g in range(genes):
        by, kind = partner_kind(g % 2, turn)
        for i in range(count - by):
            if (i // by) % 2 == kind:
                a, b = g * count + i, g * count + i + by
                pairs += [(a, b), (b, a)]
    return pairs


def core_swap(x):
    return lax.ppermute(x, "gene", [(0, 1), (1, 0), (2, 3), (3, 2)])


def cost(flops, arrays):
    return pl.CostEstimate(
        flops=flops, bytes_accessed=sum(a.size * a.dtype.itemsize for a in arrays), transcendentals=0
    )


def window_origin(gene_tiles):
    me, count = lax.axis_index("peak"), lax.axis_size("peak")
    first = jnp.maximum((me - REACH) * gene_tiles, 0)
    return jnp.minimum((first // 8) * 8, count * gene_tiles - SPAN)


def query_kernel(act_ref, w_ref, q_ref):
    q_ref[...] = jnp.dot(act_ref[...], w_ref[...], preferred_element_type=F32).astype(BF16)


def query_join_kernel(act_ref, w_ref, own_ref, q_ref):
    width = w_ref.shape[1]
    q_ref[:, :width] = own_ref[...]
    q_ref[:, width:] = jnp.dot(act_ref[...], w_ref[...], preferred_element_type=F32).astype(BF16)


def project_queries(act, own, other):
    rows, width = act.shape[0], own.shape[1]
    half = pl.pallas_call(
        query_kernel,
        in_specs=[VMEM] * 2,
        out_specs=VMEM,
        out_shape=jax.ShapeDtypeStruct((rows, width), BF16),
        cost_estimate=cost(2 * act.size * width, [act, own]),
        compiler_params=PARAMS,
        name="project_queries",
    )(act, own)
    return pl.pallas_call(
        query_join_kernel,
        in_specs=[VMEM] * 3,
        out_specs=VMEM,
        out_shape=jax.ShapeDtypeStruct((rows, 2 * width), BF16),
        cost_estimate=cost(8_000_000_000, [act, own]),
        compiler_params=PARAMS,
        name="join_queries",
    )(act, other, half)


def kv_kernel(
    gene_tiles, act_ref, wk1, wk2, wv1, wv2, mask_hbm, gene_hbm, peak_hbm,
    k_ref, v_ref, runs_ref, gene_ref, peak_ref, mask_ref, turned_ref, sems,
):
    me = lax.axis_index("peak")
    tiles = peak_ref.shape[0]
    origin = pl.multiple_of(window_origin(gene_tiles), 8)
    per_block = TILE // tiles
    columns = pl.multiple_of((me // per_block) * TILE, TILE)
    copies = [
        pltpu.make_async_copy(
            mask_hbm.at[pl.ds(origin, SPAN), pl.ds(columns, TILE)], mask_ref, sems.at[0]
        ),
        pltpu.make_async_copy(gene_hbm.at[pl.ds(origin, SPAN), :], gene_ref, sems.at[1]),
        pltpu.make_async_copy(
            peak_hbm.at[pl.ds(pl.multiple_of(me * tiles, 8), tiles), :], peak_ref, sems.at[2]
        ),
    ]
    for copy in copies:
        copy.start()
    width = wk1.shape[1]

    def block(i, carry):
        rows = pl.ds(pl.multiple_of(i * CHUNK, CHUNK), CHUNK)
        act = act_ref[rows, :]
        k_ref[rows, :width] = jnp.dot(act, wk1[...], preferred_element_type=F32).astype(BF16)
        v_ref[rows, :width] = jnp.dot(act, wv1[...], preferred_element_type=F32).astype(BF16)
        k_ref[rows, width:] = jnp.dot(act, wk2[...], preferred_element_type=F32).astype(BF16)
        v_ref[rows, width:] = jnp.dot(act, wv2[...], preferred_element_type=F32).astype(BF16)
        return carry

    lax.fori_loop(0, act_ref.shape[0] // CHUNK, block, 0)
    for copy in copies:
        copy.wait()
    blank = jnp.zeros((TILE - SPAN, TILE), I32)
    turned_ref[...] = jnp.concatenate([mask_ref[...], blank], 0).T
    allowed = turned_ref[pl.ds(pl.multiple_of((me % per_block) * tiles, 8), tiles), :]
    tags = jnp.concatenate([gene_ref[...], blank], 0).T
    peak = peak_ref[...]
    live = (
        (allowed > 0) & (tags[:1, :] <= peak[:, TILE - 1 :]) & (peak[:, :1] <= tags[TILE - 1 :, :])
    )
    place = lax.broadcasted_iota(I32, live.shape, 0)
    runs_ref[...] = jnp.zeros_like(runs_ref)
    runs_ref[0:1, :] = jnp.min(jnp.where(live, place, tiles), axis=0, keepdims=True)
    runs_ref[1:2, :] = jnp.max(jnp.where(live, place + 1, 0), axis=0, keepdims=True)


def project_kv(gene_tiles, act, wk, wv, mask, gene, peak):
    total, depth = act.shape
    width = 2 * wk[0].shape[1]
    tiles = total // TILE
    return pl.pallas_call(
        functools.partial(kv_kernel, gene_tiles),
        in_specs=[VMEM] * 5 + [HBM] * 3,
        out_specs=[VMEM] * 5,
        out_shape=[
            jax.ShapeDtypeStruct((total, width), BF16),
            jax.ShapeDtypeStruct((total, width), BF16),
            jax.ShapeDtypeStruct((8, TILE), I32),
            jax.ShapeDtypeStruct((SPAN, TILE), I32),
            jax.ShapeDtypeStruct((tiles, TILE), I32),
        ],
        scratch_shapes=[
            pltpu.VMEM((SPAN, TILE), I32),
            pltpu.VMEM((TILE, TILE), I32),
            pltpu.SemaphoreType.DMA((3,)),
        ],
        cost_estimate=cost(4 * total * depth * width, [act, act]),
        compiler_params=PARAMS,
        name="project_kv",
    )(act, *wk, *wv, mask, gene, peak)


def attend_kernel(
    turn, heads, part, runs_ref, own_bias, other_bias, gene_ref, peak_ref, q_ref, k_ref, v_ref, o_ref, acc
):
    tiles = o_ref.shape[0] // TILE
    taken = slice(part * tiles * TILE, (part + 1) * tiles * TILE)
    per_chunk = CHUNK // TILE
    dim = TILE
    scale = 0.5 / math.sqrt(dim)
    me, count = lax.axis_index("peak"), lax.axis_size("peak")
    source = me
    if turn is not None:
        by, kind = partner_kind(lax.axis_index("gene") & 1, turn)
        source = jnp.where((me // by) % 2 == kind, me + by, me - by)
    valid = (source >= 0) & (source < count)
    gene_tiles = q_ref.shape[0] // TILE
    base = jnp.where(valid, source * gene_tiles - window_origin(gene_tiles), 0) + part * tiles
    lows = [runs_ref[0, base + i] for i in range(tiles)]
    highs = [runs_ref[1, base + i] for i in range(tiles)]
    low = functools.reduce(jnp.minimum, lows)
    high = functools.reduce(jnp.maximum, highs)
    first = low // per_chunk
    last = jnp.where(valid, (high + per_chunk - 1) // per_chunk, first)
    acc[...] = jnp.zeros_like(acc)
    tags = [
        jnp.broadcast_to(gene_ref[pl.ds(base + i, 1), :], (TILE, TILE)).T for i in range(tiles)
    ]
    local = own_bias.shape[0]

    def chunk(c, carry):
        rows = pl.ds(pl.multiple_of(c * CHUNK, CHUNK), CHUNK)
        peaks = [peak_ref[pl.ds(c * per_chunk + j, 1), :] for j in range(per_chunk)]
        inside = [
            [
                jnp.where((c * per_chunk + j >= lows[i]) & (c * per_chunk + j < highs[i]), peaks[j], -1)
                for j in range(per_chunk)
            ]
            for i in range(tiles)
        ]
        for h in range(heads):
            cols = slice(h * dim, (h + 1) * dim)
            bias = own_bias[h] if h < local else other_bias[h - local]
            scores = lax.dot_general(
                q_ref[taken, cols], k_ref[rows, cols], (((1,), (1,)), ((), ())), preferred_element_type=F32
            )
            twice = jnp.tanh(scores * scale + 0.5 * bias) + 1.0
            bands = []
            for i in range(tiles):
                band = []
                for j in range(per_chunk):
                    part = twice[i * TILE : (i + 1) * TILE, j * TILE : (j + 1) * TILE]
                    band.append(jnp.where(tags[i] == inside[i][j], part, 0.0))
                bands.append(jnp.concatenate(band, 1))
            weights = jnp.concatenate(bands, 0).astype(BF16)
            acc[:, cols] += jnp.dot(weights, v_ref[rows, cols], preferred_element_type=F32)
        return carry

    lax.fori_loop(first, last, chunk, 0)
    o_ref[...] = (acc[...] * 0.5).astype(o_ref.dtype)


def attend(turn, heads, tables, q, k, v, dtype, part=0, parts=1):
    runs, own_bias, other_bias, gene, peak = tables
    shape = (q.shape[0] // parts, heads * TILE)
    return pl.pallas_call(
        functools.partial(attend_kernel, turn, heads, part),
        in_specs=[SMEM] * 3 + [VMEM] * 5,
        out_specs=VMEM,
        out_shape=jax.ShapeDtypeStruct(shape, dtype),
        scratch_shapes=[pltpu.VMEM(shape, F32)],
        cost_estimate=cost(4 * shape[0] * k.shape[0] * heads * TILE, [q, k, v, q]),
        compiler_params=PARAMS,
    )(runs, own_bias, other_bias, gene, peak, q, k, v)


def mix_kernel(part, own_ref, first_ref, second_ref, w1, w2, send_ref, keep_ref):
    rows = slice(part * send_ref.shape[0], (part + 1) * send_ref.shape[0])
    width = w1.shape[1] // 4
    depth = w1.shape[0]
    me = lax.axis_index("gene")
    first, second = first_ref[rows, :].astype(F32), second_ref[...].astype(F32)
    mine = own_ref[rows, :] + first[:, :depth] + second[:, :depth]
    theirs = first[:, depth:] + second[:, depth:]
    mine, theirs = mine.astype(BF16), theirs.astype(BF16)

    def share(block):
        cols = pl.ds(pl.multiple_of(block * width, width), width)
        return jnp.dot(mine, w1[:, cols], preferred_element_type=F32) + jnp.dot(
            theirs, w2[:, cols], preferred_element_type=F32
        )

    send_ref[:, :width] = share(me ^ 3).astype(BF16)
    send_ref[:, width:] = share(me ^ 1).astype(BF16)
    keep_ref[:, :width] = share(me ^ 2)
    keep_ref[:, width:] = share(me)


def mix(part, own, first, second, w1, w2):
    shape = (second.shape[0], w1.shape[1] // 2)
    return pl.pallas_call(
        functools.partial(mix_kernel, part),
        in_specs=[VMEM] * 5,
        out_specs=[VMEM, VMEM],
        out_shape=[jax.ShapeDtypeStruct(shape, BF16), jax.ShapeDtypeStruct(shape, F32)],
        cost_estimate=cost(4 * shape[0] * w1.size, [own, w1, w2, own, own]),
        compiler_params=PARAMS,
    )(own, first, second, w1, w2)


def finish_kernel(*refs):
    out_ref = refs[-1]
    parts = (len(refs) - 1) // 2
    rows, width = refs[parts].shape
    for part in range(parts):
        total = refs[part][:, width:] + refs[parts + part][...].astype(F32)
        out_ref[part * rows : (part + 1) * rows, :] = total.astype(BF16)


def finish(halves, others):
    rows, width = others[0].shape
    shape = (len(others) * rows, width)
    return pl.pallas_call(
        finish_kernel,
        in_specs=[VMEM] * (2 * len(others)),
        out_specs=VMEM,
        out_shape=jax.ShapeDtypeStruct(shape, BF16),
        cost_estimate=cost(2 * rows * width, halves + others),
        compiler_params=PARAMS,
        name="finish",
    )(*halves, *others)


def on_device(
    gene_act,
    peak_act,
    w_query,
    w_key,
    w_value,
    w_out,
    head_bias,
    block_mask,
    gene_chrom,
    peak_chrom,
):
    gene_tiles = gene_act.shape[0] // TILE
    local = head_bias.shape[0]
    count, genes = lax.axis_size("peak"), lax.axis_size("gene")

    def travel(x, turn):
        return lax.ppermute(x, ("gene", "peak"), swap_pairs(genes, count, turn))

    queries = project_queries(gene_act, w_query, core_swap(w_query))
    first, second = travel(queries, 0), travel(queries, 1)
    w_key = (w_key, core_swap(w_key))
    w_value = (w_value, core_swap(w_value))
    gene, peak = gene_chrom.reshape(-1, TILE), peak_chrom.reshape(-1, TILE)
    keys, values, runs, gene, peak = project_kv(
        gene_tiles, peak_act, w_key, w_value, block_mask, gene, peak
    )
    tables = (runs, head_bias, core_swap(head_bias), gene, peak)
    first = attend(0, 2 * local, tables, first, keys, values, BF16)
    first = travel(first, 0)
    seconds = []
    for part in range(PARTS):
        rows = attend(1, 2 * local, tables, second, keys, values, BF16, part, PARTS)
        seconds.append(travel(rows, 1))
    own = attend(None, local, tables, queries, keys, values, F32)
    w_other = core_swap(w_out)
    halves, others = [], []
    for part in range(PARTS):
        send, keep = mix(part, own, first, seconds[part], w_out, w_other)
        width = send.shape[1] // 2
        half = keep + core_swap(send).astype(F32)
        pairs = [(0, 2), (2, 0), (1, 3), (3, 1)]
        others.append(lax.ppermute(half[:, :width].astype(BF16), "gene", pairs))
        halves.append(half)
    return finish(halves, others)


def solution(mesh):
    placed = (
        P("peak", None),
        P("peak", None),
        P(None, "gene"),
        P(None, "gene"),
        P(None, "gene"),
        P("gene", None),
        P("gene"),
        P(),
        P(),
        P(),
    )
    return jax.shard_map(
        on_device, mesh=mesh, in_specs=placed, out_specs=P("peak", "gene"), check_vma=False
    )
```

```python
import functools
import math

import jax
import jax.numpy as jnp
from jax import lax
from jax.experimental import pallas as pl
from jax.experimental.pallas import tpu as pltpu
from jax.sharding import PartitionSpec as P


TILE = 128
REACH = 2
CHUNK = 1024
BLOCK = 512
SPAN = 32
BYS = (2, 1)
CROSSED = True
PARTS = 1
F32 = jnp.float32
BF16 = jnp.bfloat16
I32 = jnp.int32
VMEM = pl.BlockSpec(memory_space=pltpu.VMEM)
SMEM = pl.BlockSpec(memory_space=pltpu.SMEM)
HBM = pl.BlockSpec(memory_space=pltpu.HBM)
PARAMS = pltpu.CompilerParams(vmem_limit_bytes=20 << 20)


def partner_kind(core, turn):
    by = BYS[turn]
    return by, (core ^ (by - 1)) if CROSSED else core


def swap_pairs(genes, count, turn):
    pairs = []
    for g in range(genes):
        by, kind = partner_kind(g % 2, turn)
        for i in range(count - by):
            if (i // by) % 2 == kind:
                a, b = g * count + i, g * count + i + by
                pairs += [(a, b), (b, a)]
    return pairs


def core_swap(x):
    return lax.ppermute(x, "gene", [(0, 1), (1, 0), (2, 3), (3, 2)])


def cost(flops, arrays):
    return pl.CostEstimate(
        flops=flops, bytes_accessed=sum(a.size * a.dtype.itemsize for a in arrays), transcendentals=0
    )


def window_origin(gene_tiles):
    me, count = lax.axis_index("peak"), lax.axis_size("peak")
    first = jnp.maximum((me - REACH) * gene_tiles, 0)
    return jnp.minimum((first // 8) * 8, count * gene_tiles - SPAN)


def query_kernel(act_ref, w_ref, q_ref):
    q_ref[...] = jnp.dot(act_ref[...], w_ref[...], preferred_element_type=F32).astype(BF16)


def query_join_kernel(act_ref, w_ref, own_ref, q_ref):
    width = w_ref.shape[1]
    q_ref[:, :width] = own_ref[...]
    q_ref[:, width:] = jnp.dot(act_ref[...], w_ref[...], preferred_element_type=F32).astype(BF16)


def project_queries(act, own, other):
    rows, width = act.shape[0], own.shape[1]
    half = pl.pallas_call(
        query_kernel,
        in_specs=[VMEM] * 2,
        out_specs=VMEM,
        out_shape=jax.ShapeDtypeStruct((rows, width), BF16),
        cost_estimate=cost(2 * act.size * width, [act, own]),
        compiler_params=PARAMS,
        name="project_queries",
    )(act, own)
    return pl.pallas_call(
        query_join_kernel,
        in_specs=[VMEM] * 3,
        out_specs=VMEM,
        out_shape=jax.ShapeDtypeStruct((rows, 2 * width), BF16),
        cost_estimate=cost(8_000_000_000, [act, own]),
        compiler_params=PARAMS,
        name="join_queries",
    )(act, other, half)


def kv_kernel(
    gene_tiles, act_ref, wk1, wk2, wv1, wv2, mask_hbm, gene_hbm, peak_hbm,
    k_ref, v_ref, runs_ref, gene_ref, peak_ref, mask_ref, turned_ref, sems,
):
    me = lax.axis_index("peak")
    tiles = peak_ref.shape[0]
    origin = pl.multiple_of(window_origin(gene_tiles), 8)
    per_block = TILE // tiles
    columns = pl.multiple_of((me // per_block) * TILE, TILE)
    copies = [
        pltpu.make_async_copy(
            mask_hbm.at[pl.ds(origin, SPAN), pl.ds(columns, TILE)], mask_ref, sems.at[0]
        ),
        pltpu.make_async_copy(gene_hbm.at[pl.ds(origin, SPAN), :], gene_ref, sems.at[1]),
        pltpu.make_async_copy(
            peak_hbm.at[pl.ds(pl.multiple_of(me * tiles, 8), tiles), :], peak_ref, sems.at[2]
        ),
    ]
    for copy in copies:
        copy.start()
    width = wk1.shape[1]

    def block(i, carry):
        rows = pl.ds(pl.multiple_of(i * BLOCK, BLOCK), BLOCK)
        act = act_ref[rows, :]
        k_ref[rows, :width] = jnp.dot(act, wk1[...], preferred_element_type=F32).astype(BF16)
        v_ref[rows, :width] = jnp.dot(act, wv1[...], preferred_element_type=F32).astype(BF16)
        k_ref[rows, width:] = jnp.dot(act, wk2[...], preferred_element_type=F32).astype(BF16)
        v_ref[rows, width:] = jnp.dot(act, wv2[...], preferred_element_type=F32).astype(BF16)
        return carry

    lax.fori_loop(0, act_ref.shape[0] // BLOCK, block, 0)
    for copy in copies:
        copy.wait()
    blank = jnp.zeros((TILE - SPAN, TILE), I32)
    turned_ref[...] = jnp.concatenate([mask_ref[...], blank], 0).T
    allowed = turned_ref[pl.ds(pl.multiple_of((me % per_block) * tiles, 8), tiles), :]
    tags = jnp.concatenate([gene_ref[...], blank], 0).T
    peak = peak_ref[...]
    live = (
        (allowed > 0) & (tags[:1, :] <= peak[:, TILE - 1 :]) & (peak[:, :1] <= tags[TILE - 1 :, :])
    )
    place = lax.broadcasted_iota(I32, live.shape, 0)
    runs_ref[...] = jnp.zeros_like(runs_ref)
    runs_ref[0:1, :] = jnp.min(jnp.where(live, place, tiles), axis=0, keepdims=True)
    runs_ref[1:2, :] = jnp.max(jnp.where(live, place + 1, 0), axis=0, keepdims=True)


def project_kv(gene_tiles, act, wk, wv, mask, gene, peak):
    total, depth = act.shape
    width = 2 * wk[0].shape[1]
    tiles = total // TILE
    return pl.pallas_call(
        functools.partial(kv_kernel, gene_tiles),
        in_specs=[VMEM] * 5 + [HBM] * 3,
        out_specs=[VMEM] * 5,
        out_shape=[
            jax.ShapeDtypeStruct((total, width), BF16),
            jax.ShapeDtypeStruct((total, width), BF16),
            jax.ShapeDtypeStruct((8, TILE), I32),
            jax.ShapeDtypeStruct((SPAN, TILE), I32),
            jax.ShapeDtypeStruct((tiles, TILE), I32),
        ],
        scratch_shapes=[
            pltpu.VMEM((SPAN, TILE), I32),
            pltpu.VMEM((TILE, TILE), I32),
            pltpu.SemaphoreType.DMA((3,)),
        ],
        cost_estimate=cost(4 * total * depth * width, [act, act]),
        compiler_params=PARAMS,
        name="project_kv",
    )(act, *wk, *wv, mask, gene, peak)


def attend_kernel(
    turn, heads, runs_ref, own_bias, other_bias, gene_ref, peak_ref, q_ref, k_ref, v_ref, *rest
):
    *o_refs, acc = rest
    tiles = q_ref.shape[0] // TILE
    per_chunk = CHUNK // TILE
    dim = TILE
    scale = 0.5 / math.sqrt(dim)
    me, count = lax.axis_index("peak"), lax.axis_size("peak")
    source = me
    if turn is not None:
        by, kind = partner_kind(lax.axis_index("gene") & 1, turn)
        source = jnp.where((me // by) % 2 == kind, me + by, me - by)
    valid = (source >= 0) & (source < count)
    base = jnp.where(valid, source * tiles - window_origin(tiles), 0)
    lows = [runs_ref[0, base + i] for i in range(tiles)]
    highs = [runs_ref[1, base + i] for i in range(tiles)]
    low = functools.reduce(jnp.minimum, lows)
    high = functools.reduce(jnp.maximum, highs)
    first = low // per_chunk
    last = jnp.where(valid, (high + per_chunk - 1) // per_chunk, first)
    acc[...] = jnp.zeros_like(acc)
    tags = [
        jnp.broadcast_to(gene_ref[pl.ds(base + i, 1), :], (TILE, TILE)).T for i in range(tiles)
    ]
    local = own_bias.shape[0]

    def chunk(c, carry):
        rows = pl.ds(pl.multiple_of(c * CHUNK, CHUNK), CHUNK)
        peaks = [peak_ref[pl.ds(c * per_chunk + j, 1), :] for j in range(per_chunk)]
        inside = [
            [
                jnp.where((c * per_chunk + j >= lows[i]) & (c * per_chunk + j < highs[i]), peaks[j], -1)
                for j in range(per_chunk)
            ]
            for i in range(tiles)
        ]
        for h in range(heads):
            cols = slice(h * dim, (h + 1) * dim)
            bias = own_bias[h] if h < local else other_bias[h - local]
            scores = lax.dot_general(
                q_ref[:, cols], k_ref[rows, cols], (((1,), (1,)), ((), ())), preferred_element_type=F32
            )
            twice = jnp.tanh(scores * scale + 0.5 * bias) + 1.0
            bands = []
            for i in range(tiles):
                band = []
                for j in range(per_chunk):
                    part = twice[i * TILE : (i + 1) * TILE, j * TILE : (j + 1) * TILE]
                    band.append(jnp.where(tags[i] == inside[i][j], part, 0.0))
                bands.append(jnp.concatenate(band, 1))
            weights = jnp.concatenate(bands, 0).astype(BF16)
            acc[:, cols] += jnp.dot(weights, v_ref[rows, cols], preferred_element_type=F32)
        return carry

    lax.fori_loop(first, last, chunk, 0)
    size = o_refs[0].shape[0]
    for i, o_ref in enumerate(o_refs):
        o_ref[...] = (acc[i * size : (i + 1) * size, :] * 0.5).astype(o_ref.dtype)


def attend(turn, heads, tables, q, k, v, dtype, parts=1):
    runs, own_bias, other_bias, gene, peak = tables
    rows, width = q.shape[0], heads * TILE
    return pl.pallas_call(
        functools.partial(attend_kernel, turn, heads),
        in_specs=[SMEM] * 3 + [VMEM] * 5,
        out_specs=[VMEM] * parts,
        out_shape=[jax.ShapeDtypeStruct((rows // parts, width), dtype)] * parts,
        scratch_shapes=[pltpu.VMEM((rows, width), F32)],
        cost_estimate=cost(4 * rows * k.shape[0] * width, [q, k, v, q]),
        compiler_params=PARAMS,
    )(runs, own_bias, other_bias, gene, peak, q, k, v)


def mix_kernel(part, own_ref, first_ref, second_ref, w1, w2, send_ref, keep_ref):
    rows = slice(part * send_ref.shape[0], (part + 1) * send_ref.shape[0])
    width = w1.shape[1] // 4
    depth = w1.shape[0]
    me = lax.axis_index("gene")
    first, second = first_ref[rows, :].astype(F32), second_ref[...].astype(F32)
    mine = own_ref[rows, :] + first[:, :depth] + second[:, :depth]
    theirs = first[:, depth:] + second[:, depth:]
    mine, theirs = mine.astype(BF16), theirs.astype(BF16)

    def share(block):
        cols = pl.ds(pl.multiple_of(block * width, width), width)
        return jnp.dot(mine, w1[:, cols], preferred_element_type=F32) + jnp.dot(
            theirs, w2[:, cols], preferred_element_type=F32
        )

    send_ref[:, :width] = share(me ^ 3).astype(BF16)
    send_ref[:, width:] = share(me ^ 1).astype(BF16)
    keep_ref[:, :width] = share(me ^ 2)
    keep_ref[:, width:] = share(me)


def mix(part, own, first, second, w1, w2):
    shape = (second.shape[0], w1.shape[1] // 2)
    return pl.pallas_call(
        functools.partial(mix_kernel, part),
        in_specs=[VMEM] * 5,
        out_specs=[VMEM, VMEM],
        out_shape=[jax.ShapeDtypeStruct(shape, BF16), jax.ShapeDtypeStruct(shape, F32)],
        cost_estimate=cost(4 * shape[0] * w1.size, [own, w1, w2, own, own]),
        compiler_params=PARAMS,
    )(own, first, second, w1, w2)


def finish_kernel(*refs):
    out_ref = refs[-1]
    parts = (len(refs) - 1) // 2
    rows, width = refs[parts].shape
    for part in range(parts):
        total = refs[part][:, width:] + refs[parts + part][...].astype(F32)
        out_ref[part * rows : (part + 1) * rows, :] = total.astype(BF16)


def finish(halves, others):
    rows, width = others[0].shape
    shape = (len(others) * rows, width)
    return pl.pallas_call(
        finish_kernel,
        in_specs=[VMEM] * (2 * len(others)),
        out_specs=VMEM,
        out_shape=jax.ShapeDtypeStruct(shape, BF16),
        cost_estimate=cost(2 * rows * width, halves + others),
        compiler_params=PARAMS,
        name="finish",
    )(*halves, *others)


def on_device(
    gene_act,
    peak_act,
    w_query,
    w_key,
    w_value,
    w_out,
    head_bias,
    block_mask,
    gene_chrom,
    peak_chrom,
):
    gene_tiles = gene_act.shape[0] // TILE
    local = head_bias.shape[0]
    count, genes = lax.axis_size("peak"), lax.axis_size("gene")

    def travel(x, turn):
        return lax.ppermute(x, ("gene", "peak"), swap_pairs(genes, count, turn))

    queries = project_queries(gene_act, w_query, core_swap(w_query))
    first, second = travel(queries, 0), travel(queries, 1)
    w_key = (w_key, core_swap(w_key))
    w_value = (w_value, core_swap(w_value))
    gene, peak = gene_chrom.reshape(-1, TILE), peak_chrom.reshape(-1, TILE)
    keys, values, runs, gene, peak = project_kv(
        gene_tiles, peak_act, w_key, w_value, block_mask, gene, peak
    )
    tables = (runs, head_bias, core_swap(head_bias), gene, peak)
    (first,) = attend(0, 2 * local, tables, first, keys, values, BF16)
    first = travel(first, 0)
    seconds = attend(1, 2 * local, tables, second, keys, values, BF16, PARTS)
    seconds = [travel(rows, 1) for rows in seconds]
    (own,) = attend(None, local, tables, queries, keys, values, F32)
    w_other = core_swap(w_out)
    halves, others = [], []
    for part in range(PARTS):
        send, keep = mix(part, own, first, seconds[part], w_out, w_other)
        width = send.shape[1] // 2
        half = keep + core_swap(send).astype(F32)
        pairs = [(0, 2), (2, 0), (1, 3), (3, 1)]
        others.append(lax.ppermute(half[:, :width].astype(BF16), "gene", pairs))
        halves.append(half)
    return finish(halves, others)


def solution(mesh):
    placed = (
        P("peak", None),
        P("peak", None),
        P(None, "gene"),
        P(None, "gene"),
        P(None, "gene"),
        P("gene", None),
        P("gene"),
        P(),
        P(),
        P(),
    )
    return jax.shard_map(
        on_device, mesh=mesh, in_specs=placed, out_specs=P("peak", "gene"), check_vma=False
    )
```

```python
import functools
import math

import jax
import jax.numpy as jnp
from jax import lax
from jax.experimental import pallas as pl
from jax.experimental.pallas import tpu as pltpu
from jax.sharding import PartitionSpec as P


TILE = 128
REACH = 2
CHUNK = 1024
BLOCK = 512
SPAN = 32
BYS = (2, 1)
CROSSED = True
PARTS = 1
F32 = jnp.float32
BF16 = jnp.bfloat16
I32 = jnp.int32
VMEM = pl.BlockSpec(memory_space=pltpu.VMEM)
SMEM = pl.BlockSpec(memory_space=pltpu.SMEM)
HBM = pl.BlockSpec(memory_space=pltpu.HBM)
PARAMS = pltpu.CompilerParams(vmem_limit_bytes=20 << 20)


def partner_kind(core, turn):
    by = BYS[turn]
    return by, (core ^ (by - 1)) if CROSSED else core


def swap_pairs(genes, count, turn):
    pairs = []
    for g in range(genes):
        by, kind = partner_kind(g % 2, turn)
        for i in range(count - by):
            if (i // by) % 2 == kind:
                a, b = g * count + i, g * count + i + by
                pairs += [(a, b), (b, a)]
    return pairs


def core_swap(x):
    return lax.ppermute(x, "gene", [(0, 1), (1, 0), (2, 3), (3, 2)])


def cost(flops, arrays):
    return pl.CostEstimate(
        flops=flops, bytes_accessed=sum(a.size * a.dtype.itemsize for a in arrays), transcendentals=0
    )


def window_origin(gene_tiles):
    me, count = lax.axis_index("peak"), lax.axis_size("peak")
    first = jnp.maximum((me - REACH) * gene_tiles, 0)
    return jnp.minimum((first // 8) * 8, count * gene_tiles - SPAN)


def query_kernel(act_ref, w_ref, q_ref):
    q_ref[...] = jnp.dot(act_ref[...], w_ref[...], preferred_element_type=F32).astype(BF16)


def query_join_kernel(act_ref, w_ref, own_ref, q_ref):
    width = w_ref.shape[1]
    q_ref[:, :width] = own_ref[...]
    q_ref[:, width:] = jnp.dot(act_ref[...], w_ref[...], preferred_element_type=F32).astype(BF16)


def project_queries(act, own, other):
    rows, width = act.shape[0], own.shape[1]
    half = pl.pallas_call(
        query_kernel,
        in_specs=[VMEM] * 2,
        out_specs=VMEM,
        out_shape=jax.ShapeDtypeStruct((rows, width), BF16),
        cost_estimate=cost(2 * act.size * width, [act, own]),
        compiler_params=PARAMS,
        name="project_queries",
    )(act, own)
    return pl.pallas_call(
        query_join_kernel,
        in_specs=[VMEM] * 3,
        out_specs=VMEM,
        out_shape=jax.ShapeDtypeStruct((rows, 2 * width), BF16),
        cost_estimate=cost(8_000_000_000, [act, own]),
        compiler_params=PARAMS,
        name="join_queries",
    )(act, other, half)


def kv_kernel(
    gene_tiles, act_ref, wk1, wk2, wv1, wv2, mask_hbm, gene_hbm, peak_hbm,
    k_ref, v_ref, runs_ref, gene_ref, peak_ref, mask_ref, turned_ref, sems,
):
    me = lax.axis_index("peak")
    tiles = peak_ref.shape[0]
    origin = pl.multiple_of(window_origin(gene_tiles), 8)
    per_block = TILE // tiles
    columns = pl.multiple_of((me // per_block) * TILE, TILE)
    copies = [
        pltpu.make_async_copy(
            mask_hbm.at[pl.ds(origin, SPAN), pl.ds(columns, TILE)], mask_ref, sems.at[0]
        ),
        pltpu.make_async_copy(gene_hbm.at[pl.ds(origin, SPAN), :], gene_ref, sems.at[1]),
        pltpu.make_async_copy(
            peak_hbm.at[pl.ds(pl.multiple_of(me * tiles, 8), tiles), :], peak_ref, sems.at[2]
        ),
    ]
    for copy in copies:
        copy.start()
    width = wk1.shape[1]

    def block(i, carry):
        rows = pl.ds(pl.multiple_of(i * BLOCK, BLOCK), BLOCK)
        act = act_ref[rows, :]
        k_ref[rows, :width] = jnp.dot(act, wk1[...], preferred_element_type=F32).astype(BF16)
        v_ref[rows, :width] = jnp.dot(act, wv1[...], preferred_element_type=F32).astype(BF16)
        k_ref[rows, width:] = jnp.dot(act, wk2[...], preferred_element_type=F32).astype(BF16)
        v_ref[rows, width:] = jnp.dot(act, wv2[...], preferred_element_type=F32).astype(BF16)
        return carry

    lax.fori_loop(0, act_ref.shape[0] // BLOCK, block, 0)
    for copy in copies:
        copy.wait()
    blank = jnp.zeros((TILE - SPAN, TILE), I32)
    turned_ref[...] = jnp.concatenate([mask_ref[...], blank], 0).T
    allowed = turned_ref[pl.ds(pl.multiple_of((me % per_block) * tiles, 8), tiles), :]
    tags = jnp.concatenate([gene_ref[...], blank], 0).T
    peak = peak_ref[...]
    live = (
        (allowed > 0) & (tags[:1, :] <= peak[:, TILE - 1 :]) & (peak[:, :1] <= tags[TILE - 1 :, :])
    )
    place = lax.broadcasted_iota(I32, live.shape, 0)
    runs_ref[...] = jnp.zeros_like(runs_ref)
    runs_ref[0:1, :] = jnp.min(jnp.where(live, place, tiles), axis=0, keepdims=True)
    runs_ref[1:2, :] = jnp.max(jnp.where(live, place + 1, 0), axis=0, keepdims=True)


def project_kv(gene_tiles, act, wk, wv, mask, gene, peak):
    total, depth = act.shape
    width = 2 * wk[0].shape[1]
    tiles = total // TILE
    return pl.pallas_call(
        functools.partial(kv_kernel, gene_tiles),
        in_specs=[VMEM] * 5 + [HBM] * 3,
        out_specs=[VMEM] * 5,
        out_shape=[
            jax.ShapeDtypeStruct((total, width), BF16),
            jax.ShapeDtypeStruct((total, width), BF16),
            jax.ShapeDtypeStruct((8, TILE), I32),
            jax.ShapeDtypeStruct((SPAN, TILE), I32),
            jax.ShapeDtypeStruct((tiles, TILE), I32),
        ],
        scratch_shapes=[
            pltpu.VMEM((SPAN, TILE), I32),
            pltpu.VMEM((TILE, TILE), I32),
            pltpu.SemaphoreType.DMA((3,)),
        ],
        cost_estimate=cost(4 * total * depth * width, [act, act]),
        compiler_params=PARAMS,
        name="project_kv",
    )(act, *wk, *wv, mask, gene, peak)


def attend_kernel(
    turn, heads, runs_ref, own_bias, other_bias, gene_ref, peak_ref, q_ref, k_ref, v_ref, *rest
):
    *o_refs, acc = rest
    tiles = q_ref.shape[0] // TILE
    per_chunk = CHUNK // TILE
    dim = TILE
    scale = 0.5 / math.sqrt(dim)
    me, count = lax.axis_index("peak"), lax.axis_size("peak")
    source = me
    if turn is not None:
        by, kind = partner_kind(lax.axis_index("gene") & 1, turn)
        source = jnp.where((me // by) % 2 == kind, me + by, me - by)
    valid = (source >= 0) & (source < count)
    base = jnp.where(valid, source * tiles - window_origin(tiles), 0)
    lows = [runs_ref[0, base + i] for i in range(tiles)]
    highs = [runs_ref[1, base + i] for i in range(tiles)]
    low = functools.reduce(jnp.minimum, lows)
    high = functools.reduce(jnp.maximum, highs)
    first = low // per_chunk
    last = jnp.where(valid, (high + per_chunk - 1) // per_chunk, first)
    acc[...] = jnp.zeros_like(acc)
    tags = [
        jnp.broadcast_to(gene_ref[pl.ds(base + i, 1), :], (TILE, TILE)).T for i in range(tiles)
    ]
    local = own_bias.shape[0]

    def chunk(c, carry):
        rows = pl.ds(pl.multiple_of(c * CHUNK, CHUNK), CHUNK)
        peaks = [peak_ref[pl.ds(c * per_chunk + j, 1), :] for j in range(per_chunk)]
        inside = [
            [
                jnp.where((c * per_chunk + j >= lows[i]) & (c * per_chunk + j < highs[i]), peaks[j], -1)
                for j in range(per_chunk)
            ]
            for i in range(tiles)
        ]
        for h in range(heads):
            cols = slice(h * dim, (h + 1) * dim)
            bias = own_bias[h] if h < local else other_bias[h - local]
            scores = lax.dot_general(
                q_ref[:, cols], k_ref[rows, cols], (((1,), (1,)), ((), ())), preferred_element_type=F32
            )
            twice = jnp.tanh(scores * scale + 0.5 * bias) + 1.0
            bands = []
            for i in range(tiles):
                band = []
                for j in range(per_chunk):
                    part = twice[i * TILE : (i + 1) * TILE, j * TILE : (j + 1) * TILE]
                    band.append(jnp.where(tags[i] == inside[i][j], part, 0.0))
                bands.append(jnp.concatenate(band, 1))
            weights = jnp.concatenate(bands, 0).astype(BF16)
            acc[:, cols] += jnp.dot(weights, v_ref[rows, cols], preferred_element_type=F32)
        return carry

    lax.fori_loop(first, last, chunk, 0)
    size = o_refs[0].shape[0]
    for i, o_ref in enumerate(o_refs):
        o_ref[...] = (acc[i * size : (i + 1) * size, :] * 0.5).astype(o_ref.dtype)


def attend(turn, heads, tables, q, k, v, dtype, parts=1):
    runs, own_bias, other_bias, gene, peak = tables
    rows, width = q.shape[0], heads * TILE
    return pl.pallas_call(
        functools.partial(attend_kernel, turn, heads),
        in_specs=[SMEM] * 3 + [VMEM] * 5,
        out_specs=[VMEM] * parts,
        out_shape=[jax.ShapeDtypeStruct((rows // parts, width), dtype)] * parts,
        scratch_shapes=[pltpu.VMEM((rows, width), F32)],
        cost_estimate=cost(4 * rows * k.shape[0] * width, [q, k, v, q]),
        compiler_params=PARAMS,
    )(runs, own_bias, other_bias, gene, peak, q, k, v)


def mix_kernel(across, own_ref, first_ref, second_ref, w1, w2, send_ref, keep_ref):
    width = w1.shape[1] // 4
    depth = w1.shape[0]
    me = lax.axis_index("gene")
    first, second = first_ref[...].astype(F32), second_ref[...].astype(F32)
    mine = (own_ref[...] + first[:, :depth] + second[:, :depth]).astype(BF16)
    theirs = (first[:, depth:] + second[:, depth:]).astype(BF16)

    def share(block):
        cols = pl.ds(pl.multiple_of(block * width, width), width)
        return jnp.dot(mine, w1[:, cols], preferred_element_type=F32) + jnp.dot(
            theirs, w2[:, cols], preferred_element_type=F32
        )

    send_ref[...] = share(me ^ (1 + across)).astype(BF16)
    keep_ref[...] = share(me ^ across)


def mix(across, own, first, second, w1, w2):
    shape = (own.shape[0], w1.shape[1] // 4)
    return pl.pallas_call(
        functools.partial(mix_kernel, across),
        in_specs=[VMEM] * 5,
        out_specs=[VMEM, VMEM],
        out_shape=[jax.ShapeDtypeStruct(shape, BF16), jax.ShapeDtypeStruct(shape, F32)],
        cost_estimate=cost(2 * own.shape[0] * w1.size, [own, w1, w2, own, own]),
        compiler_params=PARAMS,
        name="mix_across" if across else "mix_here",
    )(own, first, second, w1, w2)


def finish_kernel(keep_ref, core_ref, z_ref, out_ref):
    total = keep_ref[...] + core_ref[...].astype(F32) + z_ref[...].astype(F32)
    out_ref[...] = total.astype(BF16)


def finish(keep, core, z):
    return pl.pallas_call(
        finish_kernel,
        in_specs=[VMEM] * 3,
        out_specs=VMEM,
        out_shape=jax.ShapeDtypeStruct(keep.shape, BF16),
        cost_estimate=cost(2 * keep.size, [keep, core, z]),
        compiler_params=PARAMS,
        name="finish",
    )(keep, core, z)


def on_device(
    gene_act,
    peak_act,
    w_query,
    w_key,
    w_value,
    w_out,
    head_bias,
    block_mask,
    gene_chrom,
    peak_chrom,
):
    gene_tiles = gene_act.shape[0] // TILE
    local = head_bias.shape[0]
    count, genes = lax.axis_size("peak"), lax.axis_size("gene")

    def travel(x, turn):
        return lax.ppermute(x, ("gene", "peak"), swap_pairs(genes, count, turn))

    queries = project_queries(gene_act, w_query, core_swap(w_query))
    first, second = travel(queries, 0), travel(queries, 1)
    w_key = (w_key, core_swap(w_key))
    w_value = (w_value, core_swap(w_value))
    gene, peak = gene_chrom.reshape(-1, TILE), peak_chrom.reshape(-1, TILE)
    keys, values, runs, gene, peak = project_kv(
        gene_tiles, peak_act, w_key, w_value, block_mask, gene, peak
    )
    tables = (runs, head_bias, core_swap(head_bias), gene, peak)
    (first,) = attend(0, 2 * local, tables, first, keys, values, BF16)
    first = travel(first, 0)
    seconds = attend(1, 2 * local, tables, second, keys, values, BF16, PARTS)
    seconds = [travel(rows, 1) for rows in seconds]
    (own,) = attend(None, local, tables, queries, keys, values, F32)
    w_other = core_swap(w_out)
    total = (own, first, seconds[0], w_out, w_other)
    send, keep = mix(2, *total)
    half = keep + core_swap(send).astype(F32)
    pairs = [(0, 2), (2, 0), (1, 3), (3, 1)]
    other = lax.ppermute(half.astype(BF16), "gene", pairs)
    send, keep = mix(0, *total)
    return finish(keep, core_swap(send), other)


def solution(mesh):
    placed = (
        P("peak", None),
        P("peak", None),
        P(None, "gene"),
        P(None, "gene"),
        P(None, "gene"),
        P("gene", None),
        P("gene"),
        P(),
        P(),
        P(),
    )
    return jax.shard_map(
        on_device, mesh=mesh, in_specs=placed, out_specs=P("peak", "gene"), check_vma=False
    )
```

```python
import functools
import math

import jax
import jax.numpy as jnp
from jax import lax
from jax.experimental import pallas as pl
from jax.experimental.pallas import tpu as pltpu
from jax.sharding import PartitionSpec as P


TILE = 128
REACH = 2
STEPS = {None: 2048, 0: 1024, 1: 2048}
BLOCK = 512
SPAN = 32
BYS = (2, 1)
CROSSED = True
PARTS = 1
F32 = jnp.float32
BF16 = jnp.bfloat16
I32 = jnp.int32
VMEM = pl.BlockSpec(memory_space=pltpu.VMEM)
SMEM = pl.BlockSpec(memory_space=pltpu.SMEM)
HBM = pl.BlockSpec(memory_space=pltpu.HBM)
PARAMS = pltpu.CompilerParams(vmem_limit_bytes=20 << 20)


def partner_kind(core, turn):
    by = BYS[turn]
    return by, (core ^ (by - 1)) if CROSSED else core


def swap_pairs(genes, count, turn):
    pairs = []
    for g in range(genes):
        by, kind = partner_kind(g % 2, turn)
        for i in range(count - by):
            if (i // by) % 2 == kind:
                a, b = g * count + i, g * count + i + by
                pairs += [(a, b), (b, a)]
    return pairs


def core_swap(x):
    return lax.ppermute(x, "gene", [(0, 1), (1, 0), (2, 3), (3, 2)])


def cost(flops, arrays):
    return pl.CostEstimate(
        flops=flops, bytes_accessed=sum(a.size * a.dtype.itemsize for a in arrays), transcendentals=0
    )


def window_origin(gene_tiles):
    me, count = lax.axis_index("peak"), lax.axis_size("peak")
    first = jnp.maximum((me - REACH) * gene_tiles, 0)
    return jnp.minimum((first // 8) * 8, count * gene_tiles - SPAN)


def query_kernel(act_ref, w_ref, q_ref):
    q_ref[...] = jnp.dot(act_ref[...], w_ref[...], preferred_element_type=F32).astype(BF16)


def query_join_kernel(act_ref, w_ref, own_ref, q_ref):
    width = w_ref.shape[1]
    q_ref[:, :width] = own_ref[...]
    q_ref[:, width:] = jnp.dot(act_ref[...], w_ref[...], preferred_element_type=F32).astype(BF16)


def project_queries(act, own, other):
    rows, width = act.shape[0], own.shape[1]
    half = pl.pallas_call(
        query_kernel,
        in_specs=[VMEM] * 2,
        out_specs=VMEM,
        out_shape=jax.ShapeDtypeStruct((rows, width), BF16),
        cost_estimate=cost(2 * act.size * width, [act, own]),
        compiler_params=PARAMS,
        name="project_queries",
    )(act, own)
    return pl.pallas_call(
        query_join_kernel,
        in_specs=[VMEM] * 3,
        out_specs=VMEM,
        out_shape=jax.ShapeDtypeStruct((rows, 2 * width), BF16),
        cost_estimate=cost(8_000_000_000, [act, own]),
        compiler_params=PARAMS,
        name="join_queries",
    )(act, other, half)


def kv_kernel(
    gene_tiles, act_ref, wk1, wk2, wv1, wv2, mask_hbm, gene_hbm, peak_hbm,
    k_ref, v_ref, runs_ref, gene_ref, peak_ref, mask_ref, turned_ref, sems,
):
    me = lax.axis_index("peak")
    tiles = peak_ref.shape[0]
    origin = pl.multiple_of(window_origin(gene_tiles), 8)
    per_block = TILE // tiles
    columns = pl.multiple_of((me // per_block) * TILE, TILE)
    copies = [
        pltpu.make_async_copy(
            mask_hbm.at[pl.ds(origin, SPAN), pl.ds(columns, TILE)], mask_ref, sems.at[0]
        ),
        pltpu.make_async_copy(gene_hbm.at[pl.ds(origin, SPAN), :], gene_ref, sems.at[1]),
        pltpu.make_async_copy(
            peak_hbm.at[pl.ds(pl.multiple_of(me * tiles, 8), tiles), :], peak_ref, sems.at[2]
        ),
    ]
    for copy in copies:
        copy.start()
    width = wk1.shape[1]

    def block(i, carry):
        rows = pl.ds(pl.multiple_of(i * BLOCK, BLOCK), BLOCK)
        act = act_ref[rows, :]
        k_ref[rows, :width] = jnp.dot(act, wk1[...], preferred_element_type=F32).astype(BF16)
        v_ref[rows, :width] = jnp.dot(act, wv1[...], preferred_element_type=F32).astype(BF16)
        k_ref[rows, width:] = jnp.dot(act, wk2[...], preferred_element_type=F32).astype(BF16)
        v_ref[rows, width:] = jnp.dot(act, wv2[...], preferred_element_type=F32).astype(BF16)
        return carry

    lax.fori_loop(0, act_ref.shape[0] // BLOCK, block, 0)
    for copy in copies:
        copy.wait()
    blank = jnp.zeros((TILE - SPAN, TILE), I32)
    turned_ref[...] = jnp.concatenate([mask_ref[...], blank], 0).T
    allowed = turned_ref[pl.ds(pl.multiple_of((me % per_block) * tiles, 8), tiles), :]
    tags = jnp.concatenate([gene_ref[...], blank], 0).T
    peak = peak_ref[...]
    live = (
        (allowed > 0) & (tags[:1, :] <= peak[:, TILE - 1 :]) & (peak[:, :1] <= tags[TILE - 1 :, :])
    )
    place = lax.broadcasted_iota(I32, live.shape, 0)
    runs_ref[...] = jnp.zeros_like(runs_ref)
    runs_ref[0:1, :] = jnp.min(jnp.where(live, place, tiles), axis=0, keepdims=True)
    runs_ref[1:2, :] = jnp.max(jnp.where(live, place + 1, 0), axis=0, keepdims=True)


def project_kv(gene_tiles, act, wk, wv, mask, gene, peak):
    total, depth = act.shape
    width = 2 * wk[0].shape[1]
    tiles = total // TILE
    return pl.pallas_call(
        functools.partial(kv_kernel, gene_tiles),
        in_specs=[VMEM] * 5 + [HBM] * 3,
        out_specs=[VMEM] * 5,
        out_shape=[
            jax.ShapeDtypeStruct((total, width), BF16),
            jax.ShapeDtypeStruct((total, width), BF16),
            jax.ShapeDtypeStruct((8, TILE), I32),
            jax.ShapeDtypeStruct((SPAN, TILE), I32),
            jax.ShapeDtypeStruct((tiles, TILE), I32),
        ],
        scratch_shapes=[
            pltpu.VMEM((SPAN, TILE), I32),
            pltpu.VMEM((TILE, TILE), I32),
            pltpu.SemaphoreType.DMA((3,)),
        ],
        cost_estimate=cost(4 * total * depth * width, [act, act]),
        compiler_params=PARAMS,
        name="project_kv",
    )(act, *wk, *wv, mask, gene, peak)


def attend_kernel(
    turn, heads, runs_ref, own_bias, other_bias, gene_ref, peak_ref, q_ref, k_ref, v_ref, *rest
):
    *o_refs, acc = rest
    tiles = q_ref.shape[0] // TILE
    step = STEPS[turn]
    per_chunk = step // TILE
    dim = TILE
    scale = 0.5 / math.sqrt(dim)
    me, count = lax.axis_index("peak"), lax.axis_size("peak")
    source = me
    if turn is not None:
        by, kind = partner_kind(lax.axis_index("gene") & 1, turn)
        source = jnp.where((me // by) % 2 == kind, me + by, me - by)
    valid = (source >= 0) & (source < count)
    base = jnp.where(valid, source * tiles - window_origin(tiles), 0)
    lows = [runs_ref[0, base + i] for i in range(tiles)]
    highs = [runs_ref[1, base + i] for i in range(tiles)]
    low = functools.reduce(jnp.minimum, lows)
    high = functools.reduce(jnp.maximum, highs)
    first = low // per_chunk
    last = jnp.where(valid, (high + per_chunk - 1) // per_chunk, first)
    acc[...] = jnp.zeros_like(acc)
    tags = [
        jnp.broadcast_to(gene_ref[pl.ds(base + i, 1), :], (TILE, TILE)).T for i in range(tiles)
    ]
    local = own_bias.shape[0]

    def chunk(c, carry):
        rows = pl.ds(pl.multiple_of(c * step, step), step)
        peaks = [peak_ref[pl.ds(c * per_chunk + j, 1), :] for j in range(per_chunk)]
        inside = [
            [
                jnp.where((c * per_chunk + j >= lows[i]) & (c * per_chunk + j < highs[i]), peaks[j], -1)
                for j in range(per_chunk)
            ]
            for i in range(tiles)
        ]
        for h in range(heads):
            cols = slice(h * dim, (h + 1) * dim)
            bias = own_bias[h] if h < local else other_bias[h - local]
            scores = lax.dot_general(
                q_ref[:, cols], k_ref[rows, cols], (((1,), (1,)), ((), ())), preferred_element_type=F32
            )
            twice = jnp.tanh(scores * scale + 0.5 * bias) + 1.0
            bands = []
            for i in range(tiles):
                band = []
                for j in range(per_chunk):
                    part = twice[i * TILE : (i + 1) * TILE, j * TILE : (j + 1) * TILE]
                    band.append(jnp.where(tags[i] == inside[i][j], part, 0.0))
                bands.append(jnp.concatenate(band, 1))
            weights = jnp.concatenate(bands, 0).astype(BF16)
            acc[:, cols] += jnp.dot(weights, v_ref[rows, cols], preferred_element_type=F32)
        return carry

    lax.fori_loop(first, last, chunk, 0)
    size = o_refs[0].shape[0]
    for i, o_ref in enumerate(o_refs):
        o_ref[...] = (acc[i * size : (i + 1) * size, :] * 0.5).astype(o_ref.dtype)


def attend(turn, heads, tables, q, k, v, dtype, parts=1):
    runs, own_bias, other_bias, gene, peak = tables
    rows, width = q.shape[0], heads * TILE
    return pl.pallas_call(
        functools.partial(attend_kernel, turn, heads),
        in_specs=[SMEM] * 3 + [VMEM] * 5,
        out_specs=[VMEM] * parts,
        out_shape=[jax.ShapeDtypeStruct((rows // parts, width), dtype)] * parts,
        scratch_shapes=[pltpu.VMEM((rows, width), F32)],
        cost_estimate=cost(4 * rows * k.shape[0] * width, [q, k, v, q]),
        compiler_params=PARAMS,
    )(runs, own_bias, other_bias, gene, peak, q, k, v)


def mix_kernel(across, own_ref, first_ref, second_ref, w1, w2, send_ref, keep_ref):
    width = w1.shape[1] // 4
    depth = w1.shape[0]
    me = lax.axis_index("gene")
    first, second = first_ref[...].astype(F32), second_ref[...].astype(F32)
    mine = (own_ref[...] + first[:, :depth] + second[:, :depth]).astype(BF16)
    theirs = (first[:, depth:] + second[:, depth:]).astype(BF16)

    def share(block):
        cols = pl.ds(pl.multiple_of(block * width, width), width)
        return jnp.dot(mine, w1[:, cols], preferred_element_type=F32) + jnp.dot(
            theirs, w2[:, cols], preferred_element_type=F32
        )

    send_ref[...] = share(me ^ (1 + across)).astype(BF16)
    keep_ref[...] = share(me ^ across)


def mix(across, own, first, second, w1, w2):
    shape = (own.shape[0], w1.shape[1] // 4)
    return pl.pallas_call(
        functools.partial(mix_kernel, across),
        in_specs=[VMEM] * 5,
        out_specs=[VMEM, VMEM],
        out_shape=[jax.ShapeDtypeStruct(shape, BF16), jax.ShapeDtypeStruct(shape, F32)],
        cost_estimate=cost(2 * own.shape[0] * w1.size, [own, w1, w2, own, own]),
        compiler_params=PARAMS,
        name="mix_across" if across else "mix_here",
    )(own, first, second, w1, w2)


def finish_kernel(keep_ref, core_ref, z_ref, out_ref):
    total = keep_ref[...] + core_ref[...].astype(F32) + z_ref[...].astype(F32)
    out_ref[...] = total.astype(BF16)


def finish(keep, core, z):
    return pl.pallas_call(
        finish_kernel,
        in_specs=[VMEM] * 3,
        out_specs=VMEM,
        out_shape=jax.ShapeDtypeStruct(keep.shape, BF16),
        cost_estimate=cost(2 * keep.size, [keep, core, z]),
        compiler_params=PARAMS,
        name="finish",
    )(keep, core, z)


def on_device(
    gene_act,
    peak_act,
    w_query,
    w_key,
    w_value,
    w_out,
    head_bias,
    block_mask,
    gene_chrom,
    peak_chrom,
):
    gene_tiles = gene_act.shape[0] // TILE
    local = head_bias.shape[0]
    count, genes = lax.axis_size("peak"), lax.axis_size("gene")

    def travel(x, turn):
        return lax.ppermute(x, ("gene", "peak"), swap_pairs(genes, count, turn))

    queries = project_queries(gene_act, w_query, core_swap(w_query))
    first, second = travel(queries, 0), travel(queries, 1)
    w_key = (w_key, core_swap(w_key))
    w_value = (w_value, core_swap(w_value))
    gene, peak = gene_chrom.reshape(-1, TILE), peak_chrom.reshape(-1, TILE)
    keys, values, runs, gene, peak = project_kv(
        gene_tiles, peak_act, w_key, w_value, block_mask, gene, peak
    )
    tables = (runs, head_bias, core_swap(head_bias), gene, peak)
    (first,) = attend(0, 2 * local, tables, first, keys, values, BF16)
    first = travel(first, 0)
    seconds = attend(1, 2 * local, tables, second, keys, values, BF16, PARTS)
    seconds = [travel(rows, 1) for rows in seconds]
    (own,) = attend(None, local, tables, queries, keys, values, F32)
    w_other = core_swap(w_out)
    total = (own, first, seconds[0], w_out, w_other)
    send, keep = mix(2, *total)
    half = keep + core_swap(send).astype(F32)
    pairs = [(0, 2), (2, 0), (1, 3), (3, 1)]
    other = lax.ppermute(half.astype(BF16), "gene", pairs)
    send, keep = mix(0, *total)
    return finish(keep, core_swap(send), other)


def solution(mesh):
    placed = (
        P("peak", None),
        P("peak", None),
        P(None, "gene"),
        P(None, "gene"),
        P(None, "gene"),
        P("gene", None),
        P("gene"),
        P(),
        P(),
        P(),
    )
    return jax.shard_map(
        on_device, mesh=mesh, in_specs=placed, out_specs=P("peak", "gene"), check_vma=False
    )
```

```python
import functools
import math

import jax
import jax.numpy as jnp
from jax import lax
from jax.experimental import pallas as pl
from jax.experimental.pallas import tpu as pltpu
from jax.sharding import PartitionSpec as P


TILE = 128
REACH = 2
STEPS = {None: 2048, 0: 1024, 1: 2048}
BLOCK = 512
SPAN = 32
BYS = (2, 1)
CROSSED = True
PARTS = 1
F32 = jnp.float32
BF16 = jnp.bfloat16
I32 = jnp.int32
VMEM = pl.BlockSpec(memory_space=pltpu.VMEM)
SMEM = pl.BlockSpec(memory_space=pltpu.SMEM)
HBM = pl.BlockSpec(memory_space=pltpu.HBM)
PARAMS = pltpu.CompilerParams(vmem_limit_bytes=20 << 20)


def partner_kind(core, turn):
    by = BYS[turn]
    return by, (core ^ (by - 1)) if CROSSED else core


def swap_pairs(genes, count, turn):
    pairs = []
    for g in range(genes):
        by, kind = partner_kind(g % 2, turn)
        for i in range(count - by):
            if (i // by) % 2 == kind:
                a, b = g * count + i, g * count + i + by
                pairs += [(a, b), (b, a)]
    return pairs


def core_swap(x):
    return lax.ppermute(x, "gene", [(0, 1), (1, 0), (2, 3), (3, 2)])


def cost(flops, arrays):
    return pl.CostEstimate(
        flops=flops, bytes_accessed=sum(a.size * a.dtype.itemsize for a in arrays), transcendentals=0
    )


def window_origin(gene_tiles):
    me, count = lax.axis_index("peak"), lax.axis_size("peak")
    first = jnp.maximum((me - REACH) * gene_tiles, 0)
    return jnp.minimum((first // 8) * 8, count * gene_tiles - SPAN)


def query_kernel(act_ref, w_ref, q_ref):
    q_ref[...] = jnp.dot(act_ref[...], w_ref[...], preferred_element_type=F32).astype(BF16)


def query_join_kernel(act_ref, w_ref, own_ref, q_ref):
    width = w_ref.shape[1]
    q_ref[:, :width] = own_ref[...]
    q_ref[:, width:] = jnp.dot(act_ref[...], w_ref[...], preferred_element_type=F32).astype(BF16)


def project_queries(act, own, other):
    rows, width = act.shape[0], own.shape[1]
    half = pl.pallas_call(
        query_kernel,
        in_specs=[VMEM] * 2,
        out_specs=VMEM,
        out_shape=jax.ShapeDtypeStruct((rows, width), BF16),
        cost_estimate=cost(2 * act.size * width, [act, own]),
        compiler_params=PARAMS,
        name="project_queries",
    )(act, own)
    return pl.pallas_call(
        query_join_kernel,
        in_specs=[VMEM] * 3,
        out_specs=VMEM,
        out_shape=jax.ShapeDtypeStruct((rows, 2 * width), BF16),
        cost_estimate=cost(8_000_000_000, [act, own]),
        compiler_params=PARAMS,
        name="join_queries",
    )(act, other, half)


def kv_kernel(
    gene_tiles, act_ref, wk1, wk2, wv1, wv2, mask_hbm, gene_hbm, peak_hbm,
    k_ref, v_ref, runs_ref, gene_ref, peak_ref, mask_ref, turned_ref, sems,
):
    me = lax.axis_index("peak")
    tiles = peak_ref.shape[0]
    origin = pl.multiple_of(window_origin(gene_tiles), 8)
    per_block = TILE // tiles
    columns = pl.multiple_of((me // per_block) * TILE, TILE)
    copies = [
        pltpu.make_async_copy(
            mask_hbm.at[pl.ds(origin, SPAN), pl.ds(columns, TILE)], mask_ref, sems.at[0]
        ),
        pltpu.make_async_copy(gene_hbm.at[pl.ds(origin, SPAN), :], gene_ref, sems.at[1]),
        pltpu.make_async_copy(
            peak_hbm.at[pl.ds(pl.multiple_of(me * tiles, 8), tiles), :], peak_ref, sems.at[2]
        ),
    ]
    for copy in copies:
        copy.start()
    width = wk1.shape[1]

    def block(i, carry):
        rows = pl.ds(pl.multiple_of(i * BLOCK, BLOCK), BLOCK)
        act = act_ref[rows, :]
        k_ref[rows, :width] = jnp.dot(act, wk1[...], preferred_element_type=F32).astype(BF16)
        v_ref[rows, :width] = jnp.dot(act, wv1[...], preferred_element_type=F32).astype(BF16)
        k_ref[rows, width:] = jnp.dot(act, wk2[...], preferred_element_type=F32).astype(BF16)
        v_ref[rows, width:] = jnp.dot(act, wv2[...], preferred_element_type=F32).astype(BF16)
        return carry

    lax.fori_loop(0, act_ref.shape[0] // BLOCK, block, 0)
    for copy in copies:
        copy.wait()
    blank = jnp.zeros((TILE - SPAN, TILE), I32)
    turned_ref[...] = jnp.concatenate([mask_ref[...], blank], 0).T
    allowed = turned_ref[pl.ds(pl.multiple_of((me % per_block) * tiles, 8), tiles), :]
    tags = jnp.concatenate([gene_ref[...], blank], 0).T
    peak = peak_ref[...]
    live = (
        (allowed > 0) & (tags[:1, :] <= peak[:, TILE - 1 :]) & (peak[:, :1] <= tags[TILE - 1 :, :])
    )
    place = lax.broadcasted_iota(I32, live.shape, 0)
    runs_ref[...] = jnp.zeros_like(runs_ref)
    runs_ref[0:1, :] = jnp.min(jnp.where(live, place, tiles), axis=0, keepdims=True)
    runs_ref[1:2, :] = jnp.max(jnp.where(live, place + 1, 0), axis=0, keepdims=True)


def project_kv(gene_tiles, act, wk, wv, mask, gene, peak):
    total, depth = act.shape
    width = 2 * wk[0].shape[1]
    tiles = total // TILE
    return pl.pallas_call(
        functools.partial(kv_kernel, gene_tiles),
        in_specs=[VMEM] * 5 + [HBM] * 3,
        out_specs=[VMEM] * 5,
        out_shape=[
            jax.ShapeDtypeStruct((total, width), BF16),
            jax.ShapeDtypeStruct((total, width), BF16),
            jax.ShapeDtypeStruct((8, TILE), I32),
            jax.ShapeDtypeStruct((SPAN, TILE), I32),
            jax.ShapeDtypeStruct((tiles, TILE), I32),
        ],
        scratch_shapes=[
            pltpu.VMEM((SPAN, TILE), I32),
            pltpu.VMEM((TILE, TILE), I32),
            pltpu.SemaphoreType.DMA((3,)),
        ],
        cost_estimate=cost(4 * total * depth * width, [act, act]),
        compiler_params=PARAMS,
        name="project_kv",
    )(act, *wk, *wv, mask, gene, peak)


def attend_kernel(
    turn, heads, runs_ref, own_bias, other_bias, gene_ref, peak_ref, q_ref, k_ref, v_ref, *rest
):
    *o_refs, acc = rest
    tiles = q_ref.shape[0] // TILE
    step = STEPS[turn]
    per_chunk = step // TILE
    dim = TILE
    scale = 0.5 / math.sqrt(dim)
    me, count = lax.axis_index("peak"), lax.axis_size("peak")
    source = me
    if turn is not None:
        by, kind = partner_kind(lax.axis_index("gene") & 1, turn)
        source = jnp.where((me // by) % 2 == kind, me + by, me - by)
    valid = (source >= 0) & (source < count)
    base = jnp.where(valid, source * tiles - window_origin(tiles), 0)
    lows = [runs_ref[0, base + i] for i in range(tiles)]
    highs = [runs_ref[1, base + i] for i in range(tiles)]
    low = functools.reduce(jnp.minimum, lows)
    high = functools.reduce(jnp.maximum, highs)
    first = low // per_chunk
    last = jnp.where(valid, (high + per_chunk - 1) // per_chunk, first)
    whole = step == k_ref.shape[0]
    tags = [
        jnp.broadcast_to(gene_ref[pl.ds(base + i, 1), :], (TILE, TILE)).T for i in range(tiles)
    ]
    local = own_bias.shape[0]

    def chunk(c, carry):
        rows = slice(None) if whole else pl.ds(pl.multiple_of(c * step, step), step)
        peaks = [peak_ref[pl.ds(c * per_chunk + j, 1), :] for j in range(per_chunk)]
        inside = [
            [
                jnp.where((c * per_chunk + j >= lows[i]) & (c * per_chunk + j < highs[i]), peaks[j], -1)
                for j in range(per_chunk)
            ]
            for i in range(tiles)
        ]
        for h in range(heads):
            cols = slice(h * dim, (h + 1) * dim)
            bias = own_bias[h] if h < local else other_bias[h - local]
            scores = lax.dot_general(
                q_ref[:, cols], k_ref[rows, cols], (((1,), (1,)), ((), ())), preferred_element_type=F32
            )
            twice = jnp.tanh(scores * scale + 0.5 * bias) + 1.0
            bands = []
            for i in range(tiles):
                band = []
                for j in range(per_chunk):
                    part = twice[i * TILE : (i + 1) * TILE, j * TILE : (j + 1) * TILE]
                    band.append(jnp.where(tags[i] == inside[i][j], part, 0.0))
                bands.append(jnp.concatenate(band, 1))
            weights = jnp.concatenate(bands, 0).astype(BF16)
            part = jnp.dot(weights, v_ref[rows, cols], preferred_element_type=F32)
            if whole:
                o_refs[0][:, cols] = (part * 0.5).astype(o_refs[0].dtype)
            else:
                acc[:, cols] += part
        return carry

    if whole:

        @pl.when(last > first)
        def _():
            chunk(0, 0)

        @pl.when(last <= first)
        def _():
            o_refs[0][...] = jnp.zeros_like(o_refs[0])

        return
    acc[...] = jnp.zeros_like(acc)
    lax.fori_loop(first, last, chunk, 0)
    size = o_refs[0].shape[0]
    for i, o_ref in enumerate(o_refs):
        o_ref[...] = (acc[i * size : (i + 1) * size, :] * 0.5).astype(o_ref.dtype)


def attend(turn, heads, tables, q, k, v, dtype, parts=1):
    runs, own_bias, other_bias, gene, peak = tables
    rows, width = q.shape[0], heads * TILE
    return pl.pallas_call(
        functools.partial(attend_kernel, turn, heads),
        in_specs=[SMEM] * 3 + [VMEM] * 5,
        out_specs=[VMEM] * parts,
        out_shape=[jax.ShapeDtypeStruct((rows // parts, width), dtype)] * parts,
        scratch_shapes=[pltpu.VMEM((rows, width), F32)],
        cost_estimate=cost(4 * rows * k.shape[0] * width, [q, k, v, q]),
        compiler_params=PARAMS,
    )(runs, own_bias, other_bias, gene, peak, q, k, v)


def mix_kernel(across, own_ref, first_ref, second_ref, w1, w2, send_ref, keep_ref):
    width = w1.shape[1] // 4
    depth = w1.shape[0]
    me = lax.axis_index("gene")
    first, second = first_ref[...].astype(F32), second_ref[...].astype(F32)
    mine = (own_ref[...] + first[:, :depth] + second[:, :depth]).astype(BF16)
    theirs = (first[:, depth:] + second[:, depth:]).astype(BF16)

    def share(block):
        cols = pl.ds(pl.multiple_of(block * width, width), width)
        return jnp.dot(mine, w1[:, cols], preferred_element_type=F32) + jnp.dot(
            theirs, w2[:, cols], preferred_element_type=F32
        )

    send_ref[...] = share(me ^ (1 + across)).astype(BF16)
    keep_ref[...] = share(me ^ across)


def mix(across, own, first, second, w1, w2):
    shape = (own.shape[0], w1.shape[1] // 4)
    return pl.pallas_call(
        functools.partial(mix_kernel, across),
        in_specs=[VMEM] * 5,
        out_specs=[VMEM, VMEM],
        out_shape=[jax.ShapeDtypeStruct(shape, BF16), jax.ShapeDtypeStruct(shape, F32)],
        cost_estimate=cost(2 * own.shape[0] * w1.size, [own, w1, w2, own, own]),
        compiler_params=PARAMS,
        name="mix_across" if across else "mix_here",
    )(own, first, second, w1, w2)


def finish_kernel(keep_ref, core_ref, z_ref, out_ref):
    total = keep_ref[...] + core_ref[...].astype(F32) + z_ref[...].astype(F32)
    out_ref[...] = total.astype(BF16)


def finish(keep, core, z):
    return pl.pallas_call(
        finish_kernel,
        in_specs=[VMEM] * 3,
        out_specs=VMEM,
        out_shape=jax.ShapeDtypeStruct(keep.shape, BF16),
        cost_estimate=cost(2 * keep.size, [keep, core, z]),
        compiler_params=PARAMS,
        name="finish",
    )(keep, core, z)


def on_device(
    gene_act,
    peak_act,
    w_query,
    w_key,
    w_value,
    w_out,
    head_bias,
    block_mask,
    gene_chrom,
    peak_chrom,
):
    gene_tiles = gene_act.shape[0] // TILE
    local = head_bias.shape[0]
    count, genes = lax.axis_size("peak"), lax.axis_size("gene")

    def travel(x, turn):
        return lax.ppermute(x, ("gene", "peak"), swap_pairs(genes, count, turn))

    queries = project_queries(gene_act, w_query, core_swap(w_query))
    first, second = travel(queries, 0), travel(queries, 1)
    w_key = (w_key, core_swap(w_key))
    w_value = (w_value, core_swap(w_value))
    gene, peak = gene_chrom.reshape(-1, TILE), peak_chrom.reshape(-1, TILE)
    keys, values, runs, gene, peak = project_kv(
        gene_tiles, peak_act, w_key, w_value, block_mask, gene, peak
    )
    tables = (runs, head_bias, core_swap(head_bias), gene, peak)
    (first,) = attend(0, 2 * local, tables, first, keys, values, BF16)
    first = travel(first, 0)
    seconds = attend(1, 2 * local, tables, second, keys, values, BF16, PARTS)
    seconds = [travel(rows, 1) for rows in seconds]
    (own,) = attend(None, local, tables, queries, keys, values, F32)
    w_other = core_swap(w_out)
    total = (own, first, seconds[0], w_out, w_other)
    send, keep = mix(2, *total)
    half = keep + core_swap(send).astype(F32)
    pairs = [(0, 2), (2, 0), (1, 3), (3, 1)]
    other = lax.ppermute(half.astype(BF16), "gene", pairs)
    send, keep = mix(0, *total)
    return finish(keep, core_swap(send), other)


def solution(mesh):
    placed = (
        P("peak", None),
        P("peak", None),
        P(None, "gene"),
        P(None, "gene"),
        P(None, "gene"),
        P("gene", None),
        P("gene"),
        P(),
        P(),
        P(),
    )
    return jax.shard_map(
        on_device, mesh=mesh, in_specs=placed, out_specs=P("peak", "gene"), check_vma=False
    )
```
